128 devices in a mesh: seq: 16 (over x, y), head: 8 (over z, core).
Axes of the slice: x: 4, y: 4, z: 4, core: 2. Of those that a mesh axis runs over, the one named last changes fastest.
Arguments:
- query: bfloat16 [12288, 8192], P('seq', 'head'), may hold values from -6 to 6
- key_in: bfloat16 [12288, 8192], P('seq', 'head'), may hold values from -6 to 6
- value: bfloat16 [12288, 8192], P('seq', 'head'), may hold values from -60 to 60
- out_grad: bfloat16 [12288, 8192], P('seq', 'head'), may hold values from -6 to 6
- gain: float32 [8192], P('head'), may hold values from 0.1 to 1.9
Outputs:
- query_grad: bfloat16 [12288, 8192], P('seq', 'head')
- key_grad: bfloat16 [12288, 8192], P('seq', 'head')
- value_grad: bfloat16 [12288, 8192], P('seq', 'head')
The draws below stay inside these ranges and needn't reach their ends.
All inputs are finite; a program needn't handle non-finite values.
Results may differ from the reference program's by a relative error of at most 0.0058.
Values sent between devices are 32-bit elements; how exact they have to be, the bound alone decides.
A program may use at most 128 MiB of HBM per device.

```python
import jax
import jax.numpy as jnp
from jax import lax

HEAD_DIM = 128
HEADS = 64
TOK_DEV = 768
TOKENS = 12288


def draw_value(key, part):
    width = HEADS * HEAD_DIM
    first, second = jax.random.split(key, 2)
    head_of = (jnp.arange(width) // HEAD_DIM).astype(jnp.float32)
    rising = 3.0 ** (head_of / max(HEADS - 1, 1))
    spread = 10.0 ** jax.random.uniform(second, (width,), jnp.float32, -0.5, 0.5)
    base = jnp.clip(jax.random.normal(first, (TOKENS, width), jnp.float32), -6.0, 6.0)
    return (base * rising * spread).astype(jnp.bfloat16)


def block_scale(stream_key, shape, shards, least, high):
    level, own = 1.0, jax.random.fold_in(stream_key, 6)
    for position, shards_of in shards:
        steps = jnp.exp(jax.random.uniform(jax.random.fold_in(own, position), (shards_of,), jnp.float32, least / len(shards), high / len(shards)))
        level = level * jnp.repeat(steps, shape[position] // shards_of).reshape([-1 if axis == position else 1 for axis in range(len(shape))])
    return level


def bell_draw(own_key, extent, scale, limit, shards=(), kind=jnp.bfloat16):
    entries = scale * jax.random.normal(own_key, extent, jnp.float32)
    if shards:
        entries = entries * block_scale(own_key, extent, shards, -0.22, 0.18)
    return jnp.clip(entries, -limit, limit).astype(kind)


def setup_inputs(seed: int = 0) -> dict:
    keys = jax.random.split(jax.random.key(seed), 6)
    query = bell_draw(keys[0], (TOKENS, HEADS * HEAD_DIM), 1.0, 6.0, ((0, 16), (1, 8)))
    key_in = bell_draw(keys[1], (TOKENS, HEADS * HEAD_DIM), 1.0, 6.0, ((0, 16), (1, 8)))
    value = draw_value(jax.random.fold_in(keys[5], 71), 0)
    out_grad = bell_draw(keys[3], (TOKENS, HEADS * HEAD_DIM), 1.0, 6.0, ((0, 16), (1, 8)))
    gain = jnp.clip(1.0 + 0.18 * jax.random.normal(keys[4], (HEADS * HEAD_DIM,), jnp.float32), 0.1, 1.9)
    return dict(query=query, key_in=key_in, value=value, out_grad=out_grad, gain=gain)


def heads_first(x):
    blocks = TOKENS // TOK_DEV
    return x.reshape(blocks, TOK_DEV, HEADS, HEAD_DIM).transpose(2, 0, 1, 3)

def tokens_first(x):
    return x.transpose(1, 2, 0, 3).reshape(TOKENS, HEADS * HEAD_DIM)

def causal_mask():
    rows = jnp.arange(TOK_DEV)[:, None]
    cols = jnp.arange(TOK_DEV)[None, :]
    return rows >= cols

def forward_head(args):
    qpart, kpart, vpart, state = args
    qf = qpart.astype(jnp.float32)
    scores = jnp.einsum('ctd,csd->cts', qf, kpart.astype(jnp.float32))
    scores = jnp.where(causal_mask()[None], scores, 0.0).astype(jnp.bfloat16)
    inner = jnp.einsum('cts,cse->cte', scores.astype(jnp.float32), vpart.astype(jnp.float32))
    outer = jnp.einsum('ctd,cde->cte', qf, state.astype(jnp.float32))
    return inner + outer

def backward_head(args):
    qpart, kpart, vpart, gpart, state, gstate = args
    qf = qpart.astype(jnp.float32)
    kf = kpart.astype(jnp.float32)
    vf = vpart.astype(jnp.float32)
    gf = gpart.astype(jnp.float32)
    mask = causal_mask()[None]
    scores = jnp.where(mask, jnp.einsum('ctd,csd->cts', qf, kf), 0.0).astype(jnp.bfloat16).astype(jnp.float32)
    gscores = jnp.where(mask, jnp.einsum('cte,cse->cts', gf, vf), 0.0).astype(jnp.bfloat16).astype(jnp.float32)
    sf = state.astype(jnp.float32)
    gsf = gstate.astype(jnp.float32)
    qgrad = jnp.einsum('cts,csd->ctd', gscores, kf) + jnp.einsum('cte,cde->ctd', gf, sf)
    kgrad = jnp.einsum('cts,ctd->csd', gscores, qf) + jnp.einsum('cse,cde->csd', vf, gsf)
    vgrad = jnp.einsum('cts,cte->cse', scores, gf) + jnp.einsum('csd,cde->cse', kf, gsf)
    return (qgrad.astype(jnp.bfloat16), kgrad.astype(jnp.bfloat16), vgrad.astype(jnp.bfloat16))

def reference(query, key_in, value, out_grad, gain):
    qh = heads_first(query)
    kh = heads_first(key_in)
    vh = heads_first(value)
    kv_local = jnp.einsum('hctd,hcte->hcde', kh.astype(jnp.float32), vh.astype(jnp.float32))
    zero_state = jnp.zeros((HEADS, 1, HEAD_DIM, HEAD_DIM), jnp.float32)
    kv_before = jnp.concatenate([zero_state, jnp.cumsum(kv_local, axis=1)[:, :-1]], axis=1).astype(jnp.bfloat16)
    attn = tokens_first(lax.map(forward_head, (qh, kh, vh, kv_before)))
    full = HEADS * HEAD_DIM
    scaled = gain[None, :] * out_grad.astype(jnp.float32)
    square_mean = lax.optimization_barrier(jnp.sum(attn * attn, axis=1)) / full
    cross_mean = lax.optimization_barrier(jnp.sum(scaled * attn, axis=1)) / full
    inv = lax.rsqrt(square_mean + 1e-06)
    attn_grad = (inv[:, None] * scaled - attn * (inv * inv * inv * cross_mean)[:, None]).astype(jnp.bfloat16)
    gh = heads_first(attn_grad)
    dkv_local = jnp.einsum('hctd,hcte->hcde', qh.astype(jnp.float32), gh.astype(jnp.float32))
    reversed_sum = jnp.cumsum(jnp.flip(dkv_local, 1), axis=1)
    dkv_after = jnp.flip(jnp.concatenate([zero_state, reversed_sum[:, :-1]], axis=1), 1).astype(jnp.bfloat16)
    qgrad, kgrad, vgrad = lax.map(backward_head, (qh, kh, vh, gh, kv_before, dkv_after))
    return (tokens_first(qgrad), tokens_first(kgrad), tokens_first(vgrad))
```

```python
import functools

import jax
import jax.numpy as jnp
from jax import lax
from jax.experimental import pallas as pl
from jax.experimental.pallas import tpu as pltpu
from jax.sharding import PartitionSpec as P

D = 128
TILE = 256
LANES = 128
EPS = 1e-06
MESH = pl.DeviceIdType.MESH
BF16 = jnp.bfloat16
F32 = jnp.float32


def dot(a, b):
    return jnp.dot(a, b, preferred_element_type=F32)


def dot_t(a, b):
    return lax.dot_general(a, b, (((1,), (1,)), ((), ())), preferred_element_type=F32)


def t_dot(a, b):
    return lax.dot_general(a, b, (((0,), (0,)), ((), ())), preferred_element_type=F32)


def remote(src, dst, send_sem, recv_sem, axis, peer):
    return pltpu.make_async_remote_copy(
        src_ref=src,
        dst_ref=dst,
        send_sem=send_sem,
        recv_sem=recv_sem,
        device_id={axis: peer},
        device_id_type=MESH,
    )


def kernel(
    blocks, peers, rows, heads,
    q_hbm, k_hbm, v_hbm, o_hbm, gain_ref,
    qg_ref, kg_ref, vg_ref,
    qb, kb, vb, ob, attn, gb, st, qt, kacc, vacc,
    local, arrived, prefix, entering, state, dstate,
    stat, stats, inv_col, coef_col,
    in_sem, out_sem, a_send, a_recv, b_send, b_recv, h_send, h_recv,
):
    me = lax.axis_index("seq")
    mine = lax.axis_index("head")
    tiles = rows // TILE
    per_head = blocks // heads
    part = D // per_head
    full = peers * heads * D

    barrier = pltpu.get_barrier_semaphore()
    for k in range(1, blocks):
        pl.semaphore_signal(
            barrier, inc=1, device_id={"seq": lax.rem(me + k, blocks)}, device_id_type=MESH
        )
    for k in range(1, peers):
        pl.semaphore_signal(
            barrier, inc=1, device_id={"head": lax.rem(mine + k, peers)}, device_id_type=MESH
        )

    def fetch(which, h):
        src = (q_hbm, k_hbm, v_hbm, o_hbm)[which]
        dst = (qb, kb, vb, ob)[which]
        return pltpu.make_async_copy(
            src.at[:, pl.ds(pl.multiple_of(h * D, D), D)], dst.at[h], in_sem.at[which, h]
        )

    first_head = me // per_head

    def rotated(i):
        return lax.rem(first_head + i, heads)

    def start_kv(i, c):
        fetch(1, rotated(i)).start()
        fetch(2, rotated(i)).start()
        return c

    def start_qo(i, c):
        fetch(0, i).start()
        return c

    def start_o(i, c):
        fetch(3, i).start()
        return c

    lax.fori_loop(0, heads, start_kv, 0)
    lax.fori_loop(0, heads, start_qo, 0)
    lax.fori_loop(0, heads, start_o, 0)

    def slice_copy(scan, s, h, half):
        return remote(
            local.at[scan, h, pl.ds(half * part, part)],
            arrived.at[scan, me],
            a_send.at[scan, s],
            a_recv.at[scan, me],
            "seq",
            s,
        )

    def send_slices(scan, h, last):
        for half in range(per_head):
            s = h * per_head + half

            @pl.when(jnp.logical_and(s != me, me != last))
            def _():
                slice_copy(scan, s, h, half).start()

            @pl.when(s == me)
            def _():
                arrived[scan, me] = local[scan, h, half * part : (half + 1) * part, :]

    def back_copy(scan, d):
        return remote(
            prefix.at[scan, d],
            entering.at[scan, me],
            b_send.at[scan, d],
            b_recv.at[scan, me],
            "seq",
            d,
        )

    def arrival(scan, j):
        return remote(
            arrived.at[scan, j], arrived.at[scan, j], a_send.at[scan, j], a_recv.at[scan, j], "seq", j
        )

    def entry(scan, s):
        return remote(
            entering.at[scan, s], entering.at[scan, s], b_send.at[scan, s], b_recv.at[scan, s], "seq", s
        )

    def scan_middle(scan, reverse):
        first = blocks - 1 if reverse else 0

        def add(i, acc):
            j = blocks - 1 - i if reverse else i
            nxt = j - 1 if reverse else j + 1

            @pl.when(j != me)
            def _():
                arrival(scan, j).wait_recv()

            acc = acc + arrived[scan, j]
            prefix[scan, nxt] = acc
            return acc

        lax.fori_loop(0, blocks - 1, add, jnp.zeros((part, D), F32))

        def send(k, c):
            d = lax.rem(me + k, blocks)

            @pl.when(d != first)
            def _():
                back_copy(scan, d).start()

            return c

        lax.fori_loop(1, blocks, send, 0)

        @pl.when(me != first)
        def _():
            entering[scan, me] = prefix[scan, me]

        @pl.when(me == first)
        def _():
            entering[scan] = jnp.zeros((blocks, part, D), F32)

    def scan_end(scan, reverse):
        first = blocks - 1 if reverse else 0

        def wait(s, c):
            @pl.when(jnp.logical_and(s != me, me != first))
            def _():
                entry(scan, s).wait_recv()

            return c

        lax.fori_loop(0, blocks, wait, 0)

    def drain(scan, reverse):
        first = blocks - 1 if reverse else 0
        last = blocks - 1 - first

        def wait(s, c):
            @pl.when(jnp.logical_and(s != me, me != last))
            def _():
                slice_copy(scan, s, s // per_head, 0).wait_send()

            @pl.when(jnp.logical_and(s != me, s != first))
            def _():
                back_copy(scan, s).wait_send()

            return c

        lax.fori_loop(0, blocks, wait, 0)

    def incoming(scan, h):
        return entering[scan, pl.ds(h * per_head, per_head)].reshape(D, D).astype(BF16)

    def kv_head(i, c):
        h = rotated(i)
        fetch(1, h).wait()
        fetch(2, h).wait()
        local[0, h] = t_dot(kb[h], vb[h])
        return c

    lax.fori_loop(0, heads, kv_head, 0)
    pl.semaphore_wait(barrier, blocks - 1 + peers - 1)

    def kv_send(i, c):
        send_slices(0, rotated(i), blocks - 1)
        return c

    lax.fori_loop(0, heads, kv_send, 0)

    at_or_below = lax.broadcasted_iota(jnp.int32, (TILE, TILE), 0) >= lax.broadcasted_iota(
        jnp.int32, (TILE, TILE), 1
    )
    at_or_above = lax.broadcasted_iota(jnp.int32, (TILE, TILE), 0) <= lax.broadcasted_iota(
        jnp.int32, (TILE, TILE), 1
    )

    def span(i):
        return slice(i * TILE, (i + 1) * TILE)

    def forward_head(h, c):
        fetch(0, h).wait()
        for t in range(tiles):
            total = None
            for s in range(t + 1):
                part_scores = dot_t(qb[h, span(t)], kb[h, span(s)])
                if s == t:
                    part_scores = jnp.where(at_or_below, part_scores, 0.0)
                term = dot(part_scores.astype(BF16), vb[h, span(s)])
                total = term if total is None else total + term
            attn[h, span(t)] = total
        for s in range(tiles):
            for t in range(s, tiles):
                turned = dot_t(kb[h, span(s)], qb[h, span(t)])
                if s == t:
                    turned = jnp.where(at_or_above, turned, 0.0)
                st[h, span(s), span(t)] = turned.astype(BF16)
        qt[h] = qb[h].T
        return c

    half_heads = heads // 2
    lax.fori_loop(0, half_heads, forward_head, 0)
    scan_middle(0, False)
    lax.fori_loop(half_heads, heads, forward_head, 0)
    scan_end(0, False)

    def take_state(h, c):
        state[h] = incoming(0, h)
        fetch(3, h).wait()
        return c

    lax.fori_loop(0, heads, take_state, 0)
    stat[...] = jnp.zeros_like(stat)

    def sums(t, c):
        at = pl.ds(pl.multiple_of(t * LANES, LANES), LANES)
        square = jnp.zeros((LANES, D), F32)
        cross = jnp.zeros((LANES, D), F32)
        for h in range(heads):
            a = attn[h, at] + dot(qb[h, at], state[h])
            attn[h, at] = a
            square = square + a * a
            cross = cross + (gain_ref[h : h + 1, :] * ob[h, at].astype(F32)) * a
        stat[0, pl.ds(t, 1)] = jnp.sum(square.T, axis=0, keepdims=True)
        stat[1, pl.ds(t, 1)] = jnp.sum(cross.T, axis=0, keepdims=True)
        return c

    lax.fori_loop(0, rows // LANES, sums, 0)

    def stat_copy(peer):
        return remote(
            stat, stats.at[mine], h_send.at[peer], h_recv.at[mine], "head", peer
        )

    for k in range(1, peers):
        stat_copy(lax.rem(mine + k, peers)).start()
    stats[mine] = stat[...]
    for k in range(1, peers):
        p = lax.rem(mine + k, peers)
        remote(stats.at[p], stats.at[p], h_send.at[p], h_recv.at[p], "head", p).wait_recv()
    whole = stats[0]
    for p in range(1, peers):
        whole = whole + stats[p]
    inv = lax.rsqrt(whole[0] / full + EPS)
    coef = inv * inv * inv * (whole[1] / full)
    for t in range(rows // LANES):
        inv_col[t * LANES : (t + 1) * LANES] = jnp.broadcast_to(inv[t : t + 1], (LANES, LANES)).T
        coef_col[t * LANES : (t + 1) * LANES] = jnp.broadcast_to(coef[t : t + 1], (LANES, LANES)).T

    def grad_head(i, c):
        h = rotated(i)
        scaled = gain_ref[pl.ds(h, 1), :] * ob[h].astype(F32)
        g = (inv_col[...] * scaled - attn[h] * coef_col[...]).astype(BF16)
        gb[h] = g
        local[1, h] = dot(qt[h], g)
        send_slices(1, h, 0)
        return c

    lax.fori_loop(0, heads, grad_head, 0)

    def backward_head(h, c):
        cols = pl.ds(pl.multiple_of(h * D, D), D)
        for t in range(tiles):
            total = dot_t(gb[h, span(t)], state[h])
            for s in range(t + 1):
                part_scores = dot_t(gb[h, span(t)], vb[h, span(s)])
                if s == t:
                    part_scores = jnp.where(at_or_below, part_scores, 0.0)
                total = total + dot(part_scores.astype(BF16), kb[h, span(s)])
            qg_ref[span(t), cols] = total.astype(BF16)
        for s in range(tiles):
            k_total, v_total = None, None
            for t in range(s, tiles):
                turned = dot_t(vb[h, span(s)], gb[h, span(t)])
                if s == t:
                    turned = jnp.where(at_or_above, turned, 0.0)
                k_term = dot(turned.astype(BF16), qb[h, span(t)])
                v_term = dot(st[h, span(s), span(t)], gb[h, span(t)])
                k_total = k_term if k_total is None else k_total + k_term
                v_total = v_term if v_total is None else v_total + v_term
            kacc[h, span(s)] = k_total
            vacc[h, span(s)] = v_total
        return c

    lax.fori_loop(0, half_heads, backward_head, 0)
    scan_middle(1, True)
    lax.fori_loop(half_heads, heads, backward_head, 0)
    scan_end(1, True)

    def last_head(h, c):
        cols = pl.ds(pl.multiple_of(h * D, D), D)
        late = incoming(1, h)
        kg_ref[:, cols] = (kacc[h] + dot_t(vb[h], late)).astype(BF16)
        vg_ref[:, cols] = (vacc[h] + dot(kb[h], late)).astype(BF16)
        return c

    lax.fori_loop(0, heads, last_head, 0)
    drain(0, False)
    drain(1, True)
    for k in range(1, peers):
        stat_copy(lax.rem(mine + k, peers)).wait_send()


def shards(query, key_in, value, out_grad, gain):
    rows, width = query.shape
    heads = width // D
    blocks = lax.axis_size("seq")
    peers = lax.axis_size("head")
    part = D * heads // blocks
    grad = jax.ShapeDtypeStruct((rows, width), BF16)
    hbm = pl.BlockSpec(memory_space=pl.ANY)
    vmem = pl.BlockSpec(memory_space=pltpu.VMEM)
    stat_rows = -(-rows // LANES // 8) * 8
    dma = pltpu.SemaphoreType.DMA
    return pl.pallas_call(
        functools.partial(kernel, blocks, peers, rows, heads),
        out_shape=(grad, grad, grad),
        in_specs=[hbm, hbm, hbm, hbm, vmem],
        out_specs=(vmem, vmem, vmem),
        scratch_shapes=[
            pltpu.VMEM((heads, rows, D), BF16),
            pltpu.VMEM((heads, rows, D), BF16),
            pltpu.VMEM((heads, rows, D), BF16),
            pltpu.VMEM((heads, rows, D), BF16),
            pltpu.VMEM((heads, rows, D), F32),
            pltpu.VMEM((heads, rows, D), BF16),
            pltpu.VMEM((heads, rows, rows), BF16),
            pltpu.VMEM((heads, D, rows), BF16),
            pltpu.VMEM((heads, rows, D), F32),
            pltpu.VMEM((heads, rows, D), F32),
            pltpu.VMEM((2, heads, D, D), F32),
            pltpu.VMEM((2, blocks, part, D), F32),
            pltpu.VMEM((2, blocks, part, D), F32),
            pltpu.VMEM((2, blocks, part, D), F32),
            pltpu.VMEM((heads, D, D), BF16),
            pltpu.VMEM((heads, D, D), BF16),
            pltpu.VMEM((2, stat_rows, LANES), F32),
            pltpu.VMEM((peers, 2, stat_rows, LANES), F32),
            pltpu.VMEM((rows, LANES), F32),
            pltpu.VMEM((rows, LANES), F32),
            dma((4, heads)),
            dma((3, heads)),
            dma((2, blocks)),
            dma((2, blocks)),
            dma((2, blocks)),
            dma((2, blocks)),
            dma((peers,)),
            dma((peers,)),
        ],
        compiler_params=pltpu.CompilerParams(
            collective_id=0, has_side_effects=True, vmem_limit_bytes=56 * 1024 * 1024
        ),
    )(query, key_in, value, out_grad, gain.reshape(heads, D))


def solution(mesh):
    spec = P("seq", "head")
    return jax.shard_map(
        shards,
        mesh=mesh,
        in_specs=(spec, spec, spec, spec, P("head")),
        out_specs=(spec, spec, spec),
        check_vma=False,
    )
```

```python
import functools

import jax
import jax.numpy as jnp
from jax import lax
from jax.experimental import pallas as pl
from jax.experimental.pallas import tpu as pltpu
from jax.sharding import PartitionSpec as P

D = 128
TILE = 256
LANES = 128
EPS = 1e-06
SIDE = 4
FORWARD_SPLIT = 6
BACKWARD_SPLIT = 3
MESH = pl.DeviceIdType.MESH
BF16 = jnp.bfloat16
F32 = jnp.float32


def dot(a, b):
    return jnp.dot(a, b, preferred_element_type=F32)


def dot_t(a, b):
    return lax.dot_general(a, b, (((1,), (1,)), ((), ())), preferred_element_type=F32)


def t_dot(a, b):
    return lax.dot_general(a, b, (((0,), (0,)), ((), ())), preferred_element_type=F32)


def remote(src, dst, send_sem, recv_sem, axis, peer):
    return pltpu.make_async_remote_copy(
        src_ref=src,
        dst_ref=dst,
        send_sem=send_sem,
        recv_sem=recv_sem,
        device_id={axis: peer},
        device_id_type=MESH,
    )


def kernel(
    blocks, peers, rows, heads,
    q_hbm, k_hbm, v_hbm, o_hbm, gain_hbm,
    qg_ref, kg_ref, vg_ref,
    gain_ref, qb, kb, vb, ob, attn, gb, st, qt, kacc, vacc,
    chunk, local, arrived, prefix, entering, state, square, cross,
    stat, stats, inv_col, coef_col,
    gain_sem, in_sem, a_send, a_recv, b_send, b_recv, h_send, h_recv,
):
    me = lax.axis_index("seq")
    mine = lax.axis_index("head")
    tiles = rows // TILE
    per_head = blocks // heads
    part = D // per_head
    full = peers * heads * D
    row, col = me // SIDE, lax.rem(me, SIDE)

    barrier = pltpu.get_barrier_semaphore()
    for k in range(1, blocks):
        pl.semaphore_signal(
            barrier, inc=1, device_id={"seq": lax.rem(me + k, blocks)}, device_id_type=MESH
        )
    for k in range(1, peers):
        pl.semaphore_signal(
            barrier, inc=1, device_id={"head": lax.rem(mine + k, peers)}, device_id_type=MESH
        )

    def fetch(which, h):
        src = (q_hbm, k_hbm, v_hbm, o_hbm)[which]
        dst = (qb, kb, vb, ob)[which]
        return pltpu.make_async_copy(
            src.at[:, pl.ds(pl.multiple_of(h * D, D), D)], dst.at[h], in_sem.at[which, h]
        )

    def far_first(i):
        return jnp.where(i == 0, 2, jnp.where(i == 1, 1, jnp.where(i == 2, 3, 0)))

    rows_heads = heads // SIDE

    def leaving(i):
        there = lax.rem(row + far_first(i // rows_heads), SIDE)
        return there * rows_heads + lax.rem(i, rows_heads)

    def returning(i):
        there = lax.rem(row - far_first(i // rows_heads) + SIDE, SIDE)
        return there * rows_heads + lax.rem(i, rows_heads)

    def start_kv(i, c):
        fetch(1, leaving(i)).start()
        fetch(2, leaving(i)).start()
        return c

    def start_q(i, c):
        fetch(0, i).start()
        return c

    def start_o(i, c):
        fetch(3, i).start()
        return c

    lax.fori_loop(0, heads, start_kv, 0)
    lax.fori_loop(0, heads, start_q, 0)
    lax.fori_loop(0, heads, start_o, 0)
    fetch_gain = pltpu.make_async_copy(gain_hbm, gain_ref, gain_sem)
    fetch_gain.start()

    def slice_copy(scan, s, h, half):
        return remote(
            local.at[scan, h, pl.ds(half * part, part)],
            arrived.at[scan, me],
            a_send.at[scan, s],
            a_recv.at[scan, me],
            "seq",
            s,
        )

    def send_slices(scan, h, last):
        for half in range(per_head):
            s = h * per_head + half

            @pl.when(jnp.logical_and(s != me, me != last))
            def _():
                slice_copy(scan, s, h, half).start()

            @pl.when(s == me)
            def _():
                arrived[scan, me] = local[scan, h, half * part : (half + 1) * part, :]

    def back_copy(scan, d):
        return remote(
            prefix.at[scan, d],
            entering.at[scan, me],
            b_send.at[scan, d],
            b_recv.at[scan, me],
            "seq",
            d,
        )

    def arrival(scan, j):
        return remote(
            arrived.at[scan, j], arrived.at[scan, j], a_send.at[scan, j], a_recv.at[scan, j], "seq", j
        )

    def entry(scan, s):
        return remote(
            entering.at[scan, s], entering.at[scan, s], b_send.at[scan, s], b_recv.at[scan, s], "seq", s
        )

    def scan_middle(scan, reverse):
        first = blocks - 1 if reverse else 0

        def add(i, acc):
            j = blocks - 1 - i if reverse else i
            nxt = j - 1 if reverse else j + 1

            @pl.when(j != me)
            def _():
                arrival(scan, j).wait_recv()

            acc = acc + arrived[scan, j]
            prefix[scan, nxt] = acc
            return acc

        lax.fori_loop(0, blocks - 1, add, jnp.zeros((part, D), F32))

        def send(k, c):
            d_row = lax.rem(row + far_first(k // SIDE), SIDE)
            d_col = lax.rem(col + far_first(lax.rem(k, SIDE)), SIDE)
            d = d_row * SIDE + d_col

            @pl.when(d != first)
            def _():
                back_copy(scan, d).start()

            return c

        lax.fori_loop(0, blocks - 1, send, 0)

        @pl.when(me != first)
        def _():
            entering[scan, me] = prefix[scan, me]

        @pl.when(me == first)
        def _():
            entering[scan] = jnp.zeros((blocks, part, D), F32)

    def scan_end(scan, h, reverse):
        first = blocks - 1 if reverse else 0
        for half in range(per_head):
            s = h * per_head + half

            @pl.when(jnp.logical_and(s != me, me != first))
            def _():
                entry(scan, s).wait_recv()

        return entering[scan, pl.ds(h * per_head, per_head)].reshape(D, D)

    def drain(scan, reverse):
        first = blocks - 1 if reverse else 0
        last = blocks - 1 - first

        def wait(s, c):
            @pl.when(jnp.logical_and(s != me, me != last))
            def _():
                slice_copy(scan, s, s // per_head, 0).wait_send()

            @pl.when(jnp.logical_and(s != me, s != first))
            def _():
                back_copy(scan, s).wait_send()

            return c

        lax.fori_loop(0, blocks, wait, 0)

    def span(i):
        return slice(i * TILE, (i + 1) * TILE)

    pl.semaphore_wait(barrier, blocks - 1 + peers - 1)

    def kv_head(i, c):
        h = leaving(i)
        fetch(1, h).wait()
        fetch(2, h).wait()
        total = None
        for t in range(tiles):
            own = t_dot(kb[h, span(t)], vb[h, span(t)])
            chunk[0, h, t] = own
            total = own if total is None else total + own
        local[0, h] = total
        send_slices(0, h, blocks - 1)
        return c

    lax.fori_loop(0, heads, kv_head, 0)

    at_or_below = lax.broadcasted_iota(jnp.int32, (TILE, TILE), 0) >= lax.broadcasted_iota(
        jnp.int32, (TILE, TILE), 1
    )
    at_or_above = lax.broadcasted_iota(jnp.int32, (TILE, TILE), 0) <= lax.broadcasted_iota(
        jnp.int32, (TILE, TILE), 1
    )

    def forward_head(h, c):
        @pl.when(h == FORWARD_SPLIT)
        def _():
            scan_middle(0, False)

        fetch(0, h).wait()
        for t in range(tiles):
            q, k = qb[h, span(t)], kb[h, span(t)]
            scores = jnp.where(at_or_below, dot_t(q, k), 0.0).astype(BF16)
            attn[h, span(t)] = dot(scores, vb[h, span(t)])
            st[h, span(t)] = jnp.where(at_or_above, dot_t(k, q), 0.0).astype(BF16)
        qt[h] = qb[h].T
        return c

    lax.fori_loop(0, heads, forward_head, 0)

    fetch_gain.wait()
    square[...] = jnp.zeros_like(square)
    cross[...] = jnp.zeros_like(cross)
    stat[...] = jnp.zeros_like(stat)

    def attend(i, c):
        h = returning(i)
        before = scan_end(0, h, False)
        fetch(3, h).wait()
        scale = gain_ref[pl.ds(h, 1), :]
        for t in range(tiles):
            rounded = before.astype(BF16)
            state[h, t] = rounded
            a = attn[h, span(t)] + dot(qb[h, span(t)], rounded)
            attn[h, span(t)] = a
            square[span(t)] += a * a
            cross[span(t)] += (scale * ob[h, span(t)].astype(F32)) * a
            if t + 1 < tiles:
                before = before + chunk[0, h, t]
        return c

    lax.fori_loop(0, heads, attend, 0)
    for t in range(rows // LANES):
        at = slice(t * LANES, (t + 1) * LANES)
        stat[0, t : t + 1] = jnp.sum(square[at].T, axis=0, keepdims=True)
        stat[1, t : t + 1] = jnp.sum(cross[at].T, axis=0, keepdims=True)

    def stat_copy(peer):
        return remote(stat, stats.at[mine], h_send.at[peer], h_recv.at[mine], "head", peer)

    for k in range(1, peers):
        stat_copy(lax.rem(mine + k, peers)).start()
    stats[mine] = stat[...]
    for k in range(1, peers):
        p = lax.rem(mine + k, peers)
        remote(stats.at[p], stats.at[p], h_send.at[p], h_recv.at[p], "head", p).wait_recv()
    whole = stats[0]
    for p in range(1, peers):
        whole = whole + stats[p]
    inv = lax.rsqrt(whole[0] / full + EPS)
    coef = inv * inv * inv * (whole[1] / full)
    for t in range(rows // LANES):
        at = slice(t * LANES, (t + 1) * LANES)
        inv_col[at] = jnp.broadcast_to(inv[t : t + 1], (LANES, LANES)).T
        coef_col[at] = jnp.broadcast_to(coef[t : t + 1], (LANES, LANES)).T

    def grad_head(i, c):
        h = leaving(i)
        scale = gain_ref[pl.ds(h, 1), :]
        total = None
        for t in range(tiles):
            scaled = scale * ob[h, span(t)].astype(F32)
            g = (inv_col[span(t)] * scaled - attn[h, span(t)] * coef_col[span(t)]).astype(BF16)
            gb[h, span(t)] = g
            own = dot(qt[h, :, span(t)], g)
            chunk[1, h, t] = own
            total = own if total is None else total + own
        local[1, h] = total
        send_slices(1, h, 0)
        return c

    lax.fori_loop(0, heads, grad_head, 0)

    def backward_head(h, c):
        @pl.when(h == BACKWARD_SPLIT)
        def _():
            scan_middle(1, True)

        cols = pl.ds(pl.multiple_of(h * D, D), D)
        for t in range(tiles):
            q, k, v, g = qb[h, span(t)], kb[h, span(t)], vb[h, span(t)], gb[h, span(t)]
            scores = jnp.where(at_or_below, dot_t(g, v), 0.0).astype(BF16)
            qg_ref[span(t), cols] = (dot(scores, k) + dot_t(g, state[h, t])).astype(BF16)
            turned = jnp.where(at_or_above, dot_t(v, g), 0.0).astype(BF16)
            kacc[h, span(t)] = dot(turned, q)
            vacc[h, span(t)] = dot(st[h, span(t)], g)
        return c

    lax.fori_loop(0, heads, backward_head, 0)

    def last_head(i, c):
        h = returning(i)
        cols = pl.ds(pl.multiple_of(h * D, D), D)
        after = scan_end(1, h, True)
        for t in reversed(range(tiles)):
            late = after.astype(BF16)
            kg_ref[span(t), cols] = (kacc[h, span(t)] + dot_t(vb[h, span(t)], late)).astype(BF16)
            vg_ref[span(t), cols] = (vacc[h, span(t)] + dot(kb[h, span(t)], late)).astype(BF16)
            if t > 0:
                after = after + chunk[1, h, t]
        return c

    lax.fori_loop(0, heads, last_head, 0)
    drain(0, False)
    drain(1, True)
    for k in range(1, peers):
        stat_copy(lax.rem(mine + k, peers)).wait_send()


def write_out(q_ref, k_ref, v_ref, q_out, k_out, v_out, sems):
    copies = [
        pltpu.make_async_copy(src, dst, sems.at[i])
        for i, (src, dst) in enumerate(((q_ref, q_out), (k_ref, k_out), (v_ref, v_out)))
    ]
    for copy in copies:
        copy.start()
    for copy in copies:
        copy.wait()


def shards(query, key_in, value, out_grad, gain):
    rows, width = query.shape
    heads = width // D
    tiles = rows // TILE
    blocks = lax.axis_size("seq")
    peers = lax.axis_size("head")
    part = D * heads // blocks
    hbm = pl.BlockSpec(memory_space=pltpu.HBM)
    vmem = pl.BlockSpec(memory_space=pltpu.VMEM)
    stat_rows = -(-rows // LANES // 8) * 8
    dma = pltpu.SemaphoreType.DMA
    operands = [
        pltpu.with_memory_space_constraint(x, pltpu.HBM)
        for x in (query, key_in, value, out_grad, gain.reshape(heads, D))
    ]
    held = pl.pallas_call(
        functools.partial(kernel, blocks, peers, rows, heads),
        out_shape=(pltpu.VMEM((rows, width), BF16),) * 3,
        in_specs=[hbm] * 5,
        out_specs=(vmem, vmem, vmem),
        scratch_shapes=[
            pltpu.VMEM((heads, D), F32),
            pltpu.VMEM((heads, rows, D), BF16),
            pltpu.VMEM((heads, rows, D), BF16),
            pltpu.VMEM((heads, rows, D), BF16),
            pltpu.VMEM((heads, rows, D), BF16),
            pltpu.VMEM((heads, rows, D), F32),
            pltpu.VMEM((heads, rows, D), BF16),
            pltpu.VMEM((heads, rows, TILE), BF16),
            pltpu.VMEM((heads, D, rows), BF16),
            pltpu.VMEM((heads, rows, D), F32),
            pltpu.VMEM((heads, rows, D), F32),
            pltpu.VMEM((2, heads, tiles, D, D), F32),
            pltpu.VMEM((2, heads, D, D), F32),
            pltpu.VMEM((2, blocks, part, D), F32),
            pltpu.VMEM((2, blocks, part, D), F32),
            pltpu.VMEM((2, blocks, part, D), F32),
            pltpu.VMEM((heads, tiles, D, D), BF16),
            pltpu.VMEM((rows, D), F32),
            pltpu.VMEM((rows, D), F32),
            pltpu.VMEM((2, stat_rows, LANES), F32),
            pltpu.VMEM((peers, 2, stat_rows, LANES), F32),
            pltpu.VMEM((rows, LANES), F32),
            pltpu.VMEM((rows, LANES), F32),
            dma(()),
            dma((4, heads)),
            dma((2, blocks)),
            dma((2, blocks)),
            dma((2, blocks)),
            dma((2, blocks)),
            dma((peers,)),
            dma((peers,)),
        ],
        compiler_params=pltpu.CompilerParams(
            collective_id=0, has_side_effects=True, vmem_limit_bytes=44 * 1024 * 1024
        ),
    )(*operands)
    return pl.pallas_call(
        write_out,
        out_shape=(jax.ShapeDtypeStruct((rows, width), BF16),) * 3,
        in_specs=[vmem] * 3,
        out_specs=(hbm, hbm, hbm),
        scratch_shapes=[dma((3,))],
        compiler_params=pltpu.CompilerParams(vmem_limit_bytes=1024 * 1024),
    )(*held)


def solution(mesh):
    spec = P("seq", "head")
    return jax.shard_map(
        shards,
        mesh=mesh,
        in_specs=(spec, spec, spec, spec, P("head")),
        out_specs=(spec, spec, spec),
        check_vma=False,
    )
```

```python
import functools

import jax
import jax.numpy as jnp
from jax import lax
from jax.experimental import pallas as pl
from jax.experimental.pallas import tpu as pltpu
from jax.sharding import PartitionSpec as P

D = 128
TILE = 256
LANES = 128
EPS = 1e-06
SIDE = 4
CHUNKS = 2
FORWARD_STOPS = (5, 7)
BACKWARD_STOPS = (3, 5)
AWAY = (
    (2, 2), (2, 1), (1, 2), (2, 3), (3, 2), (1, 1), (3, 3), (1, 3),
    (3, 1), (2, 0), (0, 2), (0, 1), (1, 0), (0, 3), (3, 0),
)
MESH = pl.DeviceIdType.MESH
BF16 = jnp.bfloat16
F32 = jnp.float32


def dot(a, b):
    return jnp.dot(a, b, preferred_element_type=F32)


def dot_t(a, b):
    return lax.dot_general(a, b, (((1,), (1,)), ((), ())), preferred_element_type=F32)


def t_dot(a, b):
    return lax.dot_general(a, b, (((0,), (0,)), ((), ())), preferred_element_type=F32)


def remote(src, dst, send_sem, recv_sem, axis, peer):
    return pltpu.make_async_remote_copy(
        src_ref=src,
        dst_ref=dst,
        send_sem=send_sem,
        recv_sem=recv_sem,
        device_id={axis: peer},
        device_id_type=MESH,
    )


def kernel(
    blocks, peers, rows, heads,
    q_hbm, k_hbm, v_hbm, o_hbm, gain_hbm,
    qg_ref, kg_ref, vg_ref,
    gain_ref, qb, kb, vb, ob, attn, gb, st, qt, kacc, vacc,
    chunk, local, arrived, prefix, entering, state, square, cross,
    stat, stats, inv_col, coef_col,
    gain_sem, in_sem, a_send, a_recv, b_send, b_recv, h_send, h_recv,
):
    me = lax.axis_index("seq")
    mine = lax.axis_index("head")
    tiles = rows // TILE
    group = heads // CHUNKS
    per_head = blocks // group
    part = D // per_head
    full = peers * heads * D
    row, col = me // SIDE, lax.rem(me, SIDE)

    def fetch(which, h):
        src = (q_hbm, k_hbm, v_hbm, o_hbm)[which]
        dst = (qb, kb, vb, ob)[which]
        return pltpu.make_async_copy(
            src.at[:, pl.ds(pl.multiple_of(h * D, D), D)], dst.at[h], in_sem.at[which, h]
        )

    def away(k):
        dx, dy = AWAY[k]
        return lax.rem(row + dx, SIDE) * SIDE + lax.rem(col + dy, SIDE)

    def start_kv(i, c):
        fetch(1, i).start()
        fetch(2, i).start()
        return c

    def start_q(i, c):
        fetch(0, i).start()
        return c

    def start_o(i, c):
        fetch(3, i).start()
        return c

    lax.fori_loop(0, heads, start_kv, 0)

    barrier = pltpu.get_barrier_semaphore()
    for k in range(1, blocks):
        pl.semaphore_signal(
            barrier, inc=1, device_id={"seq": lax.rem(me + k, blocks)}, device_id_type=MESH
        )
    for k in range(1, peers):
        pl.semaphore_signal(
            barrier, inc=1, device_id={"head": lax.rem(mine + k, peers)}, device_id_type=MESH
        )

    lax.fori_loop(0, heads, start_q, 0)
    lax.fori_loop(0, heads, start_o, 0)
    fetch_gain = pltpu.make_async_copy(gain_hbm, gain_ref, gain_sem)
    fetch_gain.start()

    def slice_copy(scan, c, s):
        return remote(
            local.at[scan, c, s],
            arrived.at[scan, c, me],
            a_send.at[scan, c],
            a_recv.at[scan, c],
            "seq",
            s,
        )

    def send_slices(scan, c, last):
        @pl.when(me != last)
        def _():
            for k in range(blocks - 1):
                slice_copy(scan, c, away(k)).start()

        arrived[scan, c, me] = local[scan, c, me]

    def back_copy(scan, c, d):
        return remote(
            prefix.at[scan, c, d],
            entering.at[scan, c, me],
            b_send.at[scan, c],
            b_recv.at[scan, c],
            "seq",
            d,
        )

    def slices(ref, scan, c, count, send_sem, recv_sem):
        at = ref.at[scan, c, pl.ds(0, count)]
        return remote(at, at, send_sem.at[scan, c], recv_sem.at[scan, c], "seq", me)

    def scan_middle(scan, c, reverse):
        first = blocks - 1 if reverse else 0
        last = blocks - 1 - first
        for count, when in ((blocks - 2, me != last), (blocks - 1, me == last)):

            @pl.when(when)
            def _():
                slices(arrived, scan, c, count, a_send, a_recv).wait_recv()

        acc = None
        for i in range(blocks - 1):
            j = blocks - 1 - i if reverse else i
            acc = arrived[scan, c, j] if acc is None else acc + arrived[scan, c, j]
            prefix[scan, c, j - 1 if reverse else j + 1] = acc
        for k in range(blocks - 1):
            d = away(k)

            @pl.when(d != first)
            def _():
                back_copy(scan, c, d).start()

        @pl.when(me != first)
        def _():
            entering[scan, c, me] = prefix[scan, c, me]

        @pl.when(me == first)
        def _():
            entering[scan, c] = jnp.zeros((blocks, part, D), F32)

    def scan_end(scan, c, reverse):
        first = blocks - 1 if reverse else 0

        @pl.when(me != first)
        def _():
            slices(entering, scan, c, blocks - 1, b_send, b_recv).wait_recv()

    def drain(scan, reverse):
        first = blocks - 1 if reverse else 0
        last = blocks - 1 - first
        for c in range(CHUNKS):

            @pl.when(me != last)
            def _():
                slices(local, scan, c, blocks - 1, a_send, a_recv).wait_send()

            for count, when in ((blocks - 2, me != first), (blocks - 1, me == first)):

                @pl.when(when)
                def _():
                    slices(prefix, scan, c, count, b_send, b_recv).wait_send()

    def incoming(scan, h):
        c = h // group
        base = lax.rem(h, group) * per_head
        return entering[scan, c, pl.ds(base, per_head)].reshape(D, D)

    def keep_local(scan, h, total):
        c = h // group
        base = lax.rem(h, group) * per_head
        local[scan, c, pl.ds(base, per_head)] = total.reshape(per_head, part, D)

    def span(i):
        return slice(i * TILE, (i + 1) * TILE)

    pl.semaphore_wait(barrier, blocks - 1 + peers - 1)

    def kv_head(i, c):
        h = i
        fetch(1, h).wait()
        fetch(2, h).wait()
        total = None
        for t in range(tiles):
            own = t_dot(kb[h, span(t)], vb[h, span(t)])
            chunk[0, h, t] = own
            total = own if total is None else total + own
        keep_local(0, h, total)
        return c

    def kv_chunk(c, z):
        lax.fori_loop(c * group, (c + 1) * group, kv_head, 0)
        send_slices(0, c, blocks - 1)
        return z

    lax.fori_loop(0, CHUNKS, kv_chunk, 0)

    at_or_below = lax.broadcasted_iota(jnp.int32, (TILE, TILE), 0) >= lax.broadcasted_iota(
        jnp.int32, (TILE, TILE), 1
    )
    at_or_above = lax.broadcasted_iota(jnp.int32, (TILE, TILE), 0) <= lax.broadcasted_iota(
        jnp.int32, (TILE, TILE), 1
    )

    def forward_head(h, c):
        for chunk_of, stop in enumerate(FORWARD_STOPS):

            @pl.when(h == stop)
            def _():
                scan_middle(0, chunk_of, False)

        fetch(0, h).wait()
        for t in range(tiles):
            q, k = qb[h, span(t)], kb[h, span(t)]
            scores = jnp.where(at_or_below, dot_t(q, k), 0.0).astype(BF16)
            attn[h, span(t)] = dot(scores, vb[h, span(t)])
            st[h, span(t)] = jnp.where(at_or_above, dot_t(k, q), 0.0).astype(BF16)
        qt[h] = qb[h].T
        return c

    lax.fori_loop(0, heads, forward_head, 0)
    for chunk_of, stop in enumerate(FORWARD_STOPS):
        if stop >= heads:
            scan_middle(0, chunk_of, False)

    fetch_gain.wait()
    square[...] = jnp.zeros_like(square)
    cross[...] = jnp.zeros_like(cross)
    stat[...] = jnp.zeros_like(stat)

    def attend(h, c):
        before = incoming(0, h)
        fetch(3, h).wait()
        scale = gain_ref[pl.ds(h, 1), :]
        for t in range(tiles):
            rounded = before.astype(BF16)
            state[h, t] = rounded
            a = attn[h, span(t)] + dot(qb[h, span(t)], rounded)
            attn[h, span(t)] = a
            square[span(t)] += a * a
            cross[span(t)] += (scale * ob[h, span(t)].astype(F32)) * a
            if t + 1 < tiles:
                before = before + chunk[0, h, t]
        return c

    def attend_chunk(c, z):
        scan_end(0, c, False)
        return lax.fori_loop(c * group, (c + 1) * group, attend, z)

    lax.fori_loop(0, CHUNKS, attend_chunk, 0)
    for t in range(rows // LANES):
        at = slice(t * LANES, (t + 1) * LANES)
        stat[0, t : t + 1] = jnp.sum(square[at].T, axis=0, keepdims=True)
        stat[1, t : t + 1] = jnp.sum(cross[at].T, axis=0, keepdims=True)

    def stat_copy(peer):
        return remote(stat, stats.at[mine], h_send, h_recv, "head", peer)

    for k in range(1, peers):
        stat_copy(lax.rem(mine + k, peers)).start()
    stats[mine] = stat[...]
    others = stats.at[pl.ds(0, peers - 1)]
    remote(others, others, h_send, h_recv, "head", mine).wait_recv()
    whole = stats[0]
    for p in range(1, peers):
        whole = whole + stats[p]
    inv = lax.rsqrt(whole[0] / full + EPS)
    coef = inv * inv * inv * (whole[1] / full)
    for t in range(rows // LANES):
        at = slice(t * LANES, (t + 1) * LANES)
        inv_col[at] = jnp.broadcast_to(inv[t : t + 1], (LANES, LANES)).T
        coef_col[at] = jnp.broadcast_to(coef[t : t + 1], (LANES, LANES)).T

    def grad_head(h, c):
        scale = gain_ref[pl.ds(h, 1), :]
        total = None
        for t in range(tiles):
            scaled = scale * ob[h, span(t)].astype(F32)
            g = (inv_col[span(t)] * scaled - attn[h, span(t)] * coef_col[span(t)]).astype(BF16)
            gb[h, span(t)] = g
            own = dot(qt[h, :, span(t)], g)
            chunk[1, h, t] = own
            total = own if total is None else total + own
        keep_local(1, h, total)
        return c

    def grad_chunk(c, z):
        lax.fori_loop(c * group, (c + 1) * group, grad_head, 0)
        send_slices(1, c, 0)
        return z

    lax.fori_loop(0, CHUNKS, grad_chunk, 0)

    def backward_head(h, c):
        for chunk_of, stop in enumerate(BACKWARD_STOPS):

            @pl.when(h == stop)
            def _():
                scan_middle(1, chunk_of, True)

        cols = pl.ds(pl.multiple_of(h * D, D), D)
        for t in range(tiles):
            q, k, v, g = qb[h, span(t)], kb[h, span(t)], vb[h, span(t)], gb[h, span(t)]
            scores = jnp.where(at_or_below, dot_t(g, v), 0.0).astype(BF16)
            qg_ref[span(t), cols] = (dot(scores, k) + dot_t(g, state[h, t])).astype(BF16)
            turned = jnp.where(at_or_above, dot_t(v, g), 0.0).astype(BF16)
            kacc[h, span(t)] = dot(turned, q)
            vacc[h, span(t)] = dot(st[h, span(t)], g)
        return c

    lax.fori_loop(0, heads, backward_head, 0)
    for chunk_of, stop in enumerate(BACKWARD_STOPS):
        if stop >= heads:
            scan_middle(1, chunk_of, True)

    def last_head(h, c):
        cols = pl.ds(pl.multiple_of(h * D, D), D)
        after = incoming(1, h)
        for t in reversed(range(tiles)):
            late = after.astype(BF16)
            kg_ref[span(t), cols] = (kacc[h, span(t)] + dot_t(vb[h, span(t)], late)).astype(BF16)
            vg_ref[span(t), cols] = (vacc[h, span(t)] + dot(kb[h, span(t)], late)).astype(BF16)
            if t > 0:
                after = after + chunk[1, h, t]
        return c

    def last_chunk(c, z):
        scan_end(1, c, True)
        return lax.fori_loop(c * group, (c + 1) * group, last_head, z)

    lax.fori_loop(0, CHUNKS, last_chunk, 0)
    drain(0, False)
    drain(1, True)
    remote(others, others, h_send, h_recv, "head", mine).wait_send()


def write_out(q_ref, k_ref, v_ref, q_out, k_out, v_out, sems):
    copies = [
        pltpu.make_async_copy(src, dst, sems.at[i])
        for i, (src, dst) in enumerate(((q_ref, q_out), (k_ref, k_out), (v_ref, v_out)))
    ]
    for copy in copies:
        copy.start()
    for copy in copies:
        copy.wait()


def shards(query, key_in, value, out_grad, gain):
    rows, width = query.shape
    heads = width // D
    tiles = rows // TILE
    blocks = lax.axis_size("seq")
    peers = lax.axis_size("head")
    part = D * heads // CHUNKS // blocks
    hbm = pl.BlockSpec(memory_space=pltpu.HBM)
    vmem = pl.BlockSpec(memory_space=pltpu.VMEM)
    stat_rows = -(-rows // LANES // 8) * 8
    dma = pltpu.SemaphoreType.DMA
    operands = [
        pltpu.with_memory_space_constraint(x, pltpu.HBM)
        for x in (query, key_in, value, out_grad, gain.reshape(heads, D))
    ]
    held = pl.pallas_call(
        functools.partial(kernel, blocks, peers, rows, heads),
        out_shape=(pltpu.VMEM((rows, width), BF16),) * 3,
        in_specs=[hbm] * 5,
        out_specs=(vmem, vmem, vmem),
        scratch_shapes=[
            pltpu.VMEM((heads, D), F32),
            pltpu.VMEM((heads, rows, D), BF16),
            pltpu.VMEM((heads, rows, D), BF16),
            pltpu.VMEM((heads, rows, D), BF16),
            pltpu.VMEM((heads, rows, D), BF16),
            pltpu.VMEM((heads, rows, D), F32),
            pltpu.VMEM((heads, rows, D), BF16),
            pltpu.VMEM((heads, rows, TILE), BF16),
            pltpu.VMEM((heads, D, rows), BF16),
            pltpu.VMEM((heads, rows, D), F32),
            pltpu.VMEM((heads, rows, D), F32),
            pltpu.VMEM((2, heads, tiles, D, D), F32),
            pltpu.VMEM((2, CHUNKS, blocks, part, D), F32),
            pltpu.VMEM((2, CHUNKS, blocks, part, D), F32),
            pltpu.VMEM((2, CHUNKS, blocks, part, D), F32),
            pltpu.VMEM((2, CHUNKS, blocks, part, D), F32),
            pltpu.VMEM((heads, tiles, D, D), BF16),
            pltpu.VMEM((rows, D), F32),
            pltpu.VMEM((rows, D), F32),
            pltpu.VMEM((2, stat_rows, LANES), F32),
            pltpu.VMEM((peers, 2, stat_rows, LANES), F32),
            pltpu.VMEM((rows, LANES), F32),
            pltpu.VMEM((rows, LANES), F32),
            dma(()),
            dma((4, heads)),
            dma((2, CHUNKS)),
            dma((2, CHUNKS)),
            dma((2, CHUNKS)),
            dma((2, CHUNKS)),
            dma(()),
            dma(()),
        ],
        compiler_params=pltpu.CompilerParams(
            collective_id=0, has_side_effects=True, vmem_limit_bytes=44 * 1024 * 1024
        ),
    )(*operands)
    return pl.pallas_call(
        write_out,
        out_shape=(jax.ShapeDtypeStruct((rows, width), BF16),) * 3,
        in_specs=[vmem] * 3,
        out_specs=(hbm, hbm, hbm),
        scratch_shapes=[dma((3,))],
        compiler_params=pltpu.CompilerParams(vmem_limit_bytes=1024 * 1024),
    )(*held)


def solution(mesh):
    spec = P("seq", "head")
    return jax.shard_map(
        shards,
        mesh=mesh,
        in_specs=(spec, spec, spec, spec, P("head")),
        out_specs=(spec, spec, spec),
        check_vma=False,
    )
```

```python
import functools

import jax
import jax.numpy as jnp
from jax import lax
from jax.experimental import pallas as pl
from jax.experimental.pallas import tpu as pltpu
from jax.sharding import PartitionSpec as P

D = 128
TILE = 256
LANES = 128
EPS = 1e-06
SIDE = 4
CHUNKS = 2
STAT_ROWS = 8
FORWARD_STOPS = (5, 7)
BACKWARD_STOPS = (3, 5)
AWAY = (
    (2, 2), (2, 1), (1, 2), (2, 3), (3, 2), (1, 1), (3, 3), (1, 3),
    (3, 1), (2, 0), (0, 2), (0, 1), (1, 0), (0, 3), (3, 0),
)
MESH = pl.DeviceIdType.MESH
BF16 = jnp.bfloat16
F32 = jnp.float32


def dot(a, b):
    return jnp.dot(a, b, preferred_element_type=F32)


def dot_t(a, b):
    return lax.dot_general(a, b, (((1,), (1,)), ((), ())), preferred_element_type=F32)


def t_dot(a, b):
    return lax.dot_general(a, b, (((0,), (0,)), ((), ())), preferred_element_type=F32)


def thirds(x):
    high = x.astype(BF16)
    rest = x - high.astype(F32)
    middle = rest.astype(BF16)
    return high, middle, (rest - middle.astype(F32)).astype(BF16)


def remote(src, dst, send_sem, recv_sem, axis, peer):
    return pltpu.make_async_remote_copy(
        src_ref=src,
        dst_ref=dst,
        send_sem=send_sem,
        recv_sem=recv_sem,
        device_id={axis: peer},
        device_id_type=MESH,
    )


def kernel(
    blocks, peers, rows, heads,
    q_hbm, k_hbm, v_hbm, o_hbm, gain_hbm,
    qg_ref, kg_ref, vg_ref, kb, vb, kacc, vacc, late_ref,
    gain_ref, qb, ob, attn, gb, st, qt,
    chunk, local, arrived, prefix, entering, state, square, cross,
    stat, stats, inv_col, coef_col,
    gain_sem, in_sem, a_send, a_recv, b_send, b_recv, h_send, h_recv,
):
    me = lax.axis_index("seq")
    mine = lax.axis_index("head")
    tiles = rows // TILE
    group = heads // CHUNKS
    per_head = blocks // group
    part = D // per_head
    full = peers * heads * D
    row, col = me // SIDE, lax.rem(me, SIDE)

    def fetch(which, h):
        src = (q_hbm, k_hbm, v_hbm, o_hbm)[which]
        dst = (qb, kb, vb, ob)[which]
        return pltpu.make_async_copy(
            src.at[:, pl.ds(pl.multiple_of(h * D, D), D)], dst.at[h], in_sem.at[which, h]
        )

    def away(k):
        dx, dy = AWAY[k]
        return lax.rem(row + dx, SIDE) * SIDE + lax.rem(col + dy, SIDE)

    def start_kv(i, c):
        fetch(1, i).start()
        fetch(2, i).start()
        return c

    def start_q(i, c):
        fetch(0, i).start()
        return c

    def start_o(i, c):
        fetch(3, i).start()
        return c

    lax.fori_loop(0, heads, start_kv, 0)

    barrier = pltpu.get_barrier_semaphore()
    for k in range(1, blocks):
        pl.semaphore_signal(
            barrier, inc=1, device_id={"seq": lax.rem(me + k, blocks)}, device_id_type=MESH
        )
    for k in range(1, peers):
        pl.semaphore_signal(
            barrier, inc=1, device_id={"head": lax.rem(mine + k, peers)}, device_id_type=MESH
        )

    lax.fori_loop(0, heads, start_q, 0)
    lax.fori_loop(0, heads, start_o, 0)
    fetch_gain = pltpu.make_async_copy(gain_hbm, gain_ref, gain_sem)
    fetch_gain.start()

    def slice_copy(scan, c, s):
        return remote(
            local.at[scan, c, s],
            arrived.at[scan, c, me],
            a_send.at[scan, c],
            a_recv.at[scan, c],
            "seq",
            s,
        )

    def send_slices(scan, c, last):
        @pl.when(me != last)
        def _():
            for k in range(blocks - 1):
                slice_copy(scan, c, away(k)).start()

        arrived[scan, c, me] = local[scan, c, me]

    def back_copy(scan, c, d):
        return remote(
            prefix.at[scan, c, d],
            entering.at[scan, c, me],
            b_send.at[scan, c],
            b_recv.at[scan, c],
            "seq",
            d,
        )

    def slices(ref, scan, c, count, send_sem, recv_sem):
        at = ref.at[scan, c, pl.ds(0, count)]
        return remote(at, at, send_sem.at[scan, c], recv_sem.at[scan, c], "seq", me)

    def scan_middle(scan, c, reverse):
        first = blocks - 1 if reverse else 0
        last = blocks - 1 - first
        for count, when in ((blocks - 2, me != last), (blocks - 1, me == last)):

            @pl.when(when)
            def _():
                slices(arrived, scan, c, count, a_send, a_recv).wait_recv()

        acc = None
        for i in range(blocks - 1):
            j = blocks - 1 - i if reverse else i
            acc = arrived[scan, c, j] if acc is None else acc + arrived[scan, c, j]
            prefix[scan, c, j - 1 if reverse else j + 1] = acc
        for k in range(blocks - 1):
            d = away(k)

            @pl.when(d != first)
            def _():
                back_copy(scan, c, d).start()

        @pl.when(me != first)
        def _():
            entering[scan, c, me] = prefix[scan, c, me]

        @pl.when(me == first)
        def _():
            entering[scan, c] = jnp.zeros((blocks, part, D), F32)

    def scan_end(scan, c, reverse):
        first = blocks - 1 if reverse else 0

        @pl.when(me != first)
        def _():
            slices(entering, scan, c, blocks - 1, b_send, b_recv).wait_recv()

    def drain_out(scan, reverse):
        last = 0 if reverse else blocks - 1
        for c in range(CHUNKS):

            @pl.when(me != last)
            def _():
                slices(local, scan, c, blocks - 1, a_send, a_recv).wait_send()

    def drain_back(scan, reverse):
        first = blocks - 1 if reverse else 0
        for c in range(CHUNKS):
            for count, when in ((blocks - 2, me != first), (blocks - 1, me == first)):

                @pl.when(when)
                def _():
                    slices(prefix, scan, c, count, b_send, b_recv).wait_send()

    def incoming(scan, h):
        c = h // group
        base = lax.rem(h, group) * per_head
        return entering[scan, c, pl.ds(base, per_head)].reshape(D, D)

    def keep_local(scan, h, total):
        c = h // group
        base = lax.rem(h, group) * per_head
        local[scan, c, pl.ds(base, per_head)] = total.reshape(per_head, part, D)

    def span(i):
        return slice(i * TILE, (i + 1) * TILE)

    pl.semaphore_wait(barrier, blocks - 1 + peers - 1)

    def kv_head(i, c):
        h = i
        fetch(1, h).wait()
        fetch(2, h).wait()
        keep_local(0, h, t_dot(kb[h], vb[h]))
        return c

    def kv_chunk(c, z):
        lax.fori_loop(c * group, (c + 1) * group, kv_head, 0, unroll=True)
        send_slices(0, c, blocks - 1)
        return z

    for chunk_of in range(CHUNKS):
        kv_chunk(chunk_of, 0)

    at_or_below = lax.broadcasted_iota(jnp.int32, (TILE, TILE), 0) >= lax.broadcasted_iota(
        jnp.int32, (TILE, TILE), 1
    )
    at_or_above = lax.broadcasted_iota(jnp.int32, (TILE, TILE), 0) <= lax.broadcasted_iota(
        jnp.int32, (TILE, TILE), 1
    )

    def forward_head(h, c):
        for chunk_of, stop in enumerate(FORWARD_STOPS):

            @pl.when(h == stop)
            def _():
                scan_middle(0, chunk_of, False)

        fetch(0, h).wait()
        for t in range(tiles):
            q, k = qb[h, span(t)], kb[h, span(t)]
            scores = jnp.where(at_or_below, dot_t(q, k), 0.0).astype(BF16)
            attn[h, span(t)] = dot(scores, vb[h, span(t)])
            st[h, span(t)] = jnp.where(at_or_above, dot_t(k, q), 0.0).astype(BF16)
            if t + 1 < tiles:
                chunk[0, h, t] = t_dot(k, vb[h, span(t)])
        qt[h] = qb[h].T
        return c

    lax.fori_loop(0, heads, forward_head, 0)
    for chunk_of, stop in enumerate(FORWARD_STOPS):
        if stop >= heads:
            scan_middle(0, chunk_of, False)

    fetch_gain.wait()
    square[...] = jnp.zeros_like(square)
    stat[...] = jnp.zeros_like(stat)
    cross[...] = jnp.zeros_like(cross)

    def attend(h, c):
        before = incoming(0, h)
        fetch(3, h).wait()
        scale = gain_ref[pl.ds(h, 1), :]
        for t in range(tiles):
            rounded = before.astype(BF16)
            state[h, t] = rounded
            a = attn[h, span(t)] + dot(qb[h, span(t)], rounded)
            attn[h, span(t)] = a
            square[span(t)] += a * a
            cross[span(t)] += (scale * ob[h, span(t)].astype(F32)) * a
            if t + 1 < tiles:
                before = before + chunk[0, h, t]
        return c

    def attend_chunk(c, z):
        scan_end(0, c, False)
        return lax.fori_loop(c * group, (c + 1) * group, attend, z, unroll=True)

    for chunk_of in range(CHUNKS):
        attend_chunk(chunk_of, 0)
    for t in range(rows // LANES):
        at = slice(t * LANES, (t + 1) * LANES)
        stat[t : t + 1] = jnp.sum(square[at].T, axis=0, keepdims=True)
        stat[STAT_ROWS + t : STAT_ROWS + t + 1] = jnp.sum(cross[at].T, axis=0, keepdims=True)

    def stat_copy(peer):
        return remote(stat, stats.at[mine], h_send, h_recv, "head", peer)

    for k in range(1, peers):
        stat_copy(lax.rem(mine + k, peers)).start()
    stats[mine] = stat[...]
    others = stats.at[pl.ds(0, peers - 1)]
    remote(others, others, h_send, h_recv, "head", mine).wait_recv()
    whole = stats[0]
    for p in range(1, peers):
        whole = whole + stats[p]
    inv = lax.rsqrt(whole[:STAT_ROWS] / full + EPS)
    coef = inv * inv * inv * (whole[STAT_ROWS:] / full)
    for t in range(rows // LANES):
        at = slice(t * LANES, (t + 1) * LANES)
        inv_col[at] = jnp.broadcast_to(inv[t : t + 1], (LANES, LANES)).T
        coef_col[at] = jnp.broadcast_to(coef[t : t + 1], (LANES, LANES)).T

    def grad_head(h, c):
        scale = gain_ref[pl.ds(h, 1), :]
        for t in range(tiles):
            scaled = scale * ob[h, span(t)].astype(F32)
            g = (inv_col[span(t)] * scaled - attn[h, span(t)] * coef_col[span(t)]).astype(BF16)
            gb[h, span(t)] = g
        keep_local(1, h, dot(qt[h], gb[h]))
        return c

    def grad_chunk(c, z):
        lax.fori_loop(c * group, (c + 1) * group, grad_head, 0, unroll=True)
        send_slices(1, c, 0)
        return z

    for chunk_of in range(CHUNKS):
        grad_chunk(chunk_of, 0)

    def backward_head(h, c):
        for chunk_of, stop in enumerate(BACKWARD_STOPS):

            @pl.when(h == stop)
            def _():
                scan_middle(1, chunk_of, True)

        cols = pl.ds(pl.multiple_of(h * D, D), D)
        for t in range(tiles):
            q, k, v, g = qb[h, span(t)], kb[h, span(t)], vb[h, span(t)], gb[h, span(t)]
            scores = jnp.where(at_or_below, dot_t(g, v), 0.0).astype(BF16)
            qg_ref[span(t), cols] = (dot(scores, k) + dot_t(g, state[h, t])).astype(BF16)
            turned = jnp.where(at_or_above, dot_t(v, g), 0.0).astype(BF16)
            kacc[h, span(t)] = dot(turned, q)
            vacc[h, span(t)] = dot(st[h, span(t)], g)
            if t > 0:
                chunk[1, h, t] = dot(qt[h, :, span(t)], g)
        return c

    lax.fori_loop(0, heads, backward_head, 0)
    for chunk_of, stop in enumerate(BACKWARD_STOPS):
        if stop >= heads:
            scan_middle(1, chunk_of, True)
    drain_out(0, False)
    drain_back(0, False)
    drain_out(1, True)
    remote(others, others, h_send, h_recv, "head", mine).wait_send()

    def last_head(h, c):
        cols = pl.ds(pl.multiple_of(h * D, D), D)
        after = incoming(1, h)
        for t in reversed(range(tiles)):
            late = after.astype(BF16)
            kg_ref[span(t), cols] = (kacc[h, span(t)] + dot_t(vb[h, span(t)], late)).astype(BF16)
            vg_ref[span(t), cols] = (vacc[h, span(t)] + dot(kb[h, span(t)], late)).astype(BF16)
            if t > 0:
                after = after + chunk[1, h, t]
        return c

    scan_end(1, 0, True)
    lax.fori_loop(0, group, last_head, 0, unroll=True)
    scan_end(1, 1, True)
    for i in range(group):
        h = group + i
        after = incoming(1, h)
        for t in reversed(range(tiles)):
            late_ref[i, t] = after.astype(BF16)
            if t > 0:
                after = after + chunk[1, h, t]
    drain_back(1, True)


def finish(
    group, tiles,
    qg_ref, kg_ref, vg_ref, kb, vb, kacc, vacc, late_ref,
    q_out, k_out, v_out,
    k_rest, v_rest, sems, rest_sems,
):
    done = pl.ds(0, group * D)
    copies = [
        pltpu.make_async_copy(qg_ref, q_out, sems.at[0]),
        pltpu.make_async_copy(kg_ref, k_out.at[:, done], sems.at[1]),
        pltpu.make_async_copy(vg_ref, v_out.at[:, done], sems.at[2]),
    ]
    for copy in copies:
        copy.start()
    for i in range(group):
        h = group + i
        for t in range(tiles):
            at = slice(t * TILE, (t + 1) * TILE)
            late = late_ref[i, t]
            k_rest[i, at] = (kacc[h, at] + dot_t(vb[h, at], late)).astype(BF16)
            v_rest[i, at] = (vacc[h, at] + dot(kb[h, at], late)).astype(BF16)
        cols = pl.ds(h * D, D)
        for which, (rest, out) in enumerate(((k_rest, k_out), (v_rest, v_out))):
            copy = pltpu.make_async_copy(rest.at[i], out.at[:, cols], rest_sems.at[which, i])
            copy.start()
            copies.append(copy)
    for copy in copies:
        copy.wait()


def shards(query, key_in, value, out_grad, gain):
    rows, width = query.shape
    heads = width // D
    tiles = rows // TILE
    blocks = lax.axis_size("seq")
    peers = lax.axis_size("head")
    part = D * heads // CHUNKS // blocks
    hbm = pl.BlockSpec(memory_space=pltpu.HBM)
    vmem = pl.BlockSpec(memory_space=pltpu.VMEM)
    dma = pltpu.SemaphoreType.DMA
    operands = [
        pltpu.with_memory_space_constraint(x, pltpu.HBM)
        for x in (query, key_in, value, out_grad, gain.reshape(heads, D))
    ]
    group = heads // CHUNKS
    held_shapes = [
        pltpu.VMEM((rows, width), BF16),
        pltpu.VMEM((rows, group * D), BF16),
        pltpu.VMEM((rows, group * D), BF16),
        pltpu.VMEM((heads, rows, D), BF16),
        pltpu.VMEM((heads, rows, D), BF16),
        pltpu.VMEM((heads, rows, D), F32),
        pltpu.VMEM((heads, rows, D), F32),
        pltpu.VMEM((group, tiles, D, D), BF16),
    ]
    held = pl.pallas_call(
        functools.partial(kernel, blocks, peers, rows, heads),
        out_shape=held_shapes,
        in_specs=[hbm] * 5,
        out_specs=[vmem] * len(held_shapes),
        scratch_shapes=[
            pltpu.VMEM((heads, D), F32),
            pltpu.VMEM((heads, rows, D), BF16),
            pltpu.VMEM((heads, rows, D), BF16),
            pltpu.VMEM((heads, rows, D), F32),
            pltpu.VMEM((heads, rows, D), BF16),
            pltpu.VMEM((heads, rows, TILE), BF16),
            pltpu.VMEM((heads, D, rows), BF16),
            pltpu.VMEM((2, heads, tiles, D, D), F32),
            pltpu.VMEM((2, CHUNKS, blocks, part, D), F32),
            pltpu.VMEM((2, CHUNKS, blocks, part, D), F32),
            pltpu.VMEM((2, CHUNKS, blocks, part, D), F32),
            pltpu.VMEM((2, CHUNKS, blocks, part, D), F32),
            pltpu.VMEM((heads, tiles, D, D), BF16),
            pltpu.VMEM((rows, D), F32),
            pltpu.VMEM((rows, D), F32),
            pltpu.VMEM((2 * STAT_ROWS, LANES), F32),
            pltpu.VMEM((peers, 2 * STAT_ROWS, LANES), F32),
            pltpu.VMEM((rows, LANES), F32),
            pltpu.VMEM((rows, LANES), F32),
            dma(()),
            dma((4, heads)),
            dma((2, CHUNKS)),
            dma((2, CHUNKS)),
            dma((2, CHUNKS)),
            dma((2, CHUNKS)),
            dma(()),
            dma(()),
        ],
        compiler_params=pltpu.CompilerParams(
            collective_id=0, has_side_effects=True, vmem_limit_bytes=40 * 1024 * 1024
        ),
    )(*operands)
    return pl.pallas_call(
        functools.partial(finish, group, tiles),
        out_shape=(jax.ShapeDtypeStruct((rows, width), BF16),) * 3,
        in_specs=[vmem] * len(held_shapes),
        out_specs=(hbm, hbm, hbm),
        scratch_shapes=[
            pltpu.VMEM((group, rows, D), BF16),
            pltpu.VMEM((group, rows, D), BF16),
            dma((3,)),
            dma((2, group)),
        ],
        compiler_params=pltpu.CompilerParams(vmem_limit_bytes=4 * 1024 * 1024),
    )(*held)


def solution(mesh):
    spec = P("seq", "head")
    return jax.shard_map(
        shards,
        mesh=mesh,
        in_specs=(spec, spec, spec, spec, P("head")),
        out_specs=(spec, spec, spec),
        check_vma=False,
    )
```

```python
import functools

import jax
import jax.numpy as jnp
from jax import lax
from jax.experimental import pallas as pl
from jax.experimental.pallas import tpu as pltpu
from jax.sharding import PartitionSpec as P

D = 128
TILE = 256
LANES = 128
EPS = 1e-06
SIDE = 4
CHUNKS = 2
STAT_ROWS = 8
FORWARD_STOPS = (5, 7)
BACKWARD_STOPS = (3, 6)
AWAY = (
    (2, 2), (2, 1), (1, 2), (2, 3), (3, 2), (1, 1), (3, 3), (1, 3),
    (3, 1), (2, 0), (0, 2), (0, 1), (1, 0), (0, 3), (3, 0),
)
MESH = pl.DeviceIdType.MESH
BF16 = jnp.bfloat16
F32 = jnp.float32


def dot(a, b):
    return jnp.dot(a, b, preferred_element_type=F32)


def dot_t(a, b):
    return lax.dot_general(a, b, (((1,), (1,)), ((), ())), preferred_element_type=F32)


def t_dot(a, b):
    return lax.dot_general(a, b, (((0,), (0,)), ((), ())), preferred_element_type=F32)


def thirds(x):
    high = x.astype(BF16)
    rest = x - high.astype(F32)
    middle = rest.astype(BF16)
    return high, middle, (rest - middle.astype(F32)).astype(BF16)


def remote(src, dst, send_sem, recv_sem, axis, peer):
    return pltpu.make_async_remote_copy(
        src_ref=src,
        dst_ref=dst,
        send_sem=send_sem,
        recv_sem=recv_sem,
        device_id={axis: peer},
        device_id_type=MESH,
    )


def kernel(
    blocks, peers, rows, heads,
    q_hbm, k_hbm, v_hbm, o_hbm, gain_hbm,
    qg_ref, kg_ref, vg_ref, kb, vb, kacc, vacc, late_ref,
    gain_ref, qb, ob, attn, gb, st, qt,
    chunk, local, arrived, prefix, entering, state, square, cross,
    stat, stats, inv_col, coef_col,
    gain_sem, in_sem, a_send, a_recv, b_send, b_recv, h_send, h_recv,
):
    me = lax.axis_index("seq")
    mine = lax.axis_index("head")
    tiles = rows // TILE
    group = heads // CHUNKS
    per_head = blocks // group
    part = D // per_head
    full = peers * heads * D
    row, col = me // SIDE, lax.rem(me, SIDE)

    def fetch(which, h):
        src = (q_hbm, k_hbm, v_hbm, o_hbm)[which]
        dst = (qb, kb, vb, ob)[which]
        return pltpu.make_async_copy(
            src.at[:, pl.ds(pl.multiple_of(h * D, D), D)], dst.at[h], in_sem.at[which, h]
        )

    def away(k):
        dx, dy = AWAY[k]
        return lax.rem(row + dx, SIDE) * SIDE + lax.rem(col + dy, SIDE)

    def start_kv(i, c):
        fetch(1, i).start()
        fetch(2, i).start()
        return c

    def start_q(i, c):
        fetch(0, i).start()
        return c

    def start_o(i, c):
        fetch(3, i).start()
        return c

    fetch_gain = pltpu.make_async_copy(gain_hbm, gain_ref, gain_sem)
    barrier = pltpu.get_barrier_semaphore()
    lax.fori_loop(0, group, start_kv, 0)
    for k in range(blocks - 1):
        pl.semaphore_signal(barrier, inc=1, device_id={"seq": away(k)}, device_id_type=MESH)
    lax.fori_loop(group, heads, start_kv, 0)
    for k in range(1, peers):
        pl.semaphore_signal(
            barrier, inc=1, device_id={"head": lax.rem(mine + k, peers)}, device_id_type=MESH
        )

    def slice_copy(scan, c, s):
        return remote(
            local.at[scan, c, s],
            arrived.at[scan, c, me],
            a_send.at[scan, c],
            a_recv.at[scan, c],
            "seq",
            s,
        )

    def send_slices(scan, c, last):
        @pl.when(me != last)
        def _():
            for k in range(blocks - 1):
                slice_copy(scan, c, away(k)).start()

        arrived[scan, c, me] = local[scan, c, me]

    def back_copy(scan, c, d):
        return remote(
            prefix.at[scan, c, d],
            entering.at[scan, c, me],
            b_send.at[scan, c],
            b_recv.at[scan, c],
            "seq",
            d,
        )

    def slices(ref, scan, c, count, send_sem, recv_sem):
        at = ref.at[scan, c, pl.ds(0, count)]
        return remote(at, at, send_sem.at[scan, c], recv_sem.at[scan, c], "seq", me)

    def scan_middle(scan, c, reverse):
        first = blocks - 1 if reverse else 0
        last = blocks - 1 - first
        for count, when in ((blocks - 2, me != last), (blocks - 1, me == last)):

            @pl.when(when)
            def _():
                slices(arrived, scan, c, count, a_send, a_recv).wait_recv()

        acc = None
        for i in range(blocks - 1):
            j = blocks - 1 - i if reverse else i
            acc = arrived[scan, c, j] if acc is None else acc + arrived[scan, c, j]
            prefix[scan, c, j - 1 if reverse else j + 1] = acc
        for k in range(blocks - 1):
            d = away(k)

            @pl.when(d != first)
            def _():
                back_copy(scan, c, d).start()

        @pl.when(me != first)
        def _():
            entering[scan, c, me] = prefix[scan, c, me]

        @pl.when(me == first)
        def _():
            entering[scan, c] = jnp.zeros((blocks, part, D), F32)

    def scan_end(scan, c, reverse):
        first = blocks - 1 if reverse else 0

        @pl.when(me != first)
        def _():
            slices(entering, scan, c, blocks - 1, b_send, b_recv).wait_recv()

    def drain_out(scan, reverse):
        last = 0 if reverse else blocks - 1
        for c in range(CHUNKS):

            @pl.when(me != last)
            def _():
                slices(local, scan, c, blocks - 1, a_send, a_recv).wait_send()

    def drain_back(scan, reverse):
        first = blocks - 1 if reverse else 0
        for c in range(CHUNKS):
            for count, when in ((blocks - 2, me != first), (blocks - 1, me == first)):

                @pl.when(when)
                def _():
                    slices(prefix, scan, c, count, b_send, b_recv).wait_send()

    def incoming(scan, h):
        c = h // group
        base = lax.rem(h, group) * per_head
        return entering[scan, c, pl.ds(base, per_head)].reshape(D, D)

    def keep_local(scan, h, total):
        c = h // group
        base = lax.rem(h, group) * per_head
        local[scan, c, pl.ds(base, per_head)] = total.reshape(per_head, part, D)

    def span(i):
        return slice(i * TILE, (i + 1) * TILE)

    pl.semaphore_wait(barrier, blocks - 1 + peers - 1)

    def kv_head(i, c):
        h = i
        fetch(1, h).wait()
        fetch(2, h).wait()
        keep_local(0, h, t_dot(kb[h], vb[h]))
        return c

    def kv_chunk(c, z):
        lax.fori_loop(c * group, (c + 1) * group, kv_head, 0, unroll=True)
        send_slices(0, c, blocks - 1)
        if c == 0:
            lax.fori_loop(0, heads, start_q, 0)
        return z

    for chunk_of in range(CHUNKS):
        kv_chunk(chunk_of, 0)
    lax.fori_loop(0, heads, start_o, 0)
    fetch_gain.start()

    at_or_below = lax.broadcasted_iota(jnp.int32, (TILE, TILE), 0) >= lax.broadcasted_iota(
        jnp.int32, (TILE, TILE), 1
    )
    at_or_above = lax.broadcasted_iota(jnp.int32, (TILE, TILE), 0) <= lax.broadcasted_iota(
        jnp.int32, (TILE, TILE), 1
    )

    def forward_head(h, c):
        for chunk_of, stop in enumerate(FORWARD_STOPS):

            @pl.when(h == stop)
            def _():
                scan_middle(0, chunk_of, False)

        fetch(0, h).wait()
        for t in range(tiles):
            q, k = qb[h, span(t)], kb[h, span(t)]
            scores = jnp.where(at_or_below, dot_t(q, k), 0.0).astype(BF16)
            attn[h, span(t)] = dot(scores, vb[h, span(t)])
            st[h, span(t)] = jnp.where(at_or_above, dot_t(k, q), 0.0).astype(BF16)
            if t + 1 < tiles:
                chunk[0, h, t] = t_dot(k, vb[h, span(t)])
        qt[h] = qb[h].T
        return c

    lax.fori_loop(0, heads, forward_head, 0)
    for chunk_of, stop in enumerate(FORWARD_STOPS):
        if stop >= heads:
            scan_middle(0, chunk_of, False)

    fetch_gain.wait()
    square[...] = jnp.zeros_like(square)
    stat[...] = jnp.zeros_like(stat)
    cross[...] = jnp.zeros_like(cross)

    def attend_chunk(c):
        own = range(c * group, (c + 1) * group)
        for h in own:
            fetch(3, h).wait()
        scan_end(0, c, False)
        for h in own:
            before = incoming(0, h)
            for t in range(tiles):
                state[h, t] = before.astype(BF16)
                if t + 1 < tiles:
                    before = before + chunk[0, h, t]
        for t in range(rows // LANES):
            at = slice(t * LANES, (t + 1) * LANES)
            squares, crosses = square[at], cross[at]
            for h in own:
                a = attn[h, at] + dot(qb[h, at], state[h, t * LANES // TILE])
                attn[h, at] = a
                squares = squares + a * a
                crosses = crosses + (gain_ref[h : h + 1, :] * ob[h, at].astype(F32)) * a
            if c + 1 < CHUNKS:
                square[at] = squares
                cross[at] = crosses
            else:
                stat[t : t + 1] = jnp.sum(squares.T, axis=0, keepdims=True)
                stat[STAT_ROWS + t : STAT_ROWS + t + 1] = jnp.sum(crosses.T, axis=0, keepdims=True)

    for chunk_of in range(CHUNKS):
        attend_chunk(chunk_of)
    def stat_copy(peer):
        return remote(stat, stats.at[mine], h_send, h_recv, "head", peer)

    for k in range(1, peers):
        stat_copy(lax.rem(mine + k, peers)).start()
    stats[mine] = stat[...]
    others = stats.at[pl.ds(0, peers - 1)]
    remote(others, others, h_send, h_recv, "head", mine).wait_recv()
    whole = stats[0]
    for p in range(1, peers):
        whole = whole + stats[p]
    inv = lax.rsqrt(whole[:STAT_ROWS] / full + EPS)
    coef = inv * inv * inv * (whole[STAT_ROWS:] / full)
    def grad_chunk(c):
        own = range(c * group, (c + 1) * group)
        for t in range(rows // LANES):
            at = slice(t * LANES, (t + 1) * LANES)
            if c == 0:
                scale = jnp.broadcast_to(inv[t : t + 1], (LANES, LANES)).T
                shift = jnp.broadcast_to(coef[t : t + 1], (LANES, LANES)).T
                inv_col[at] = scale
                coef_col[at] = shift
            else:
                scale, shift = inv_col[at], coef_col[at]
            for h in own:
                scaled = gain_ref[h : h + 1, :] * ob[h, at].astype(F32)
                gb[h, at] = (scale * scaled - attn[h, at] * shift).astype(BF16)
        for h in own:
            keep_local(1, h, dot(qt[h], gb[h]))
        send_slices(1, c, 0)

    for chunk_of in range(CHUNKS):
        grad_chunk(chunk_of)

    def backward_head(h, c):
        for chunk_of, stop in enumerate(BACKWARD_STOPS):

            @pl.when(h == stop)
            def _():
                scan_middle(1, chunk_of, True)

        cols = pl.ds(pl.multiple_of(h * D, D), D)
        for t in range(tiles):
            q, k, v, g = qb[h, span(t)], kb[h, span(t)], vb[h, span(t)], gb[h, span(t)]
            scores = jnp.where(at_or_below, dot_t(g, v), 0.0).astype(BF16)
            qg_ref[span(t), cols] = (dot(scores, k) + dot_t(g, state[h, t])).astype(BF16)
            turned = jnp.where(at_or_above, dot_t(v, g), 0.0).astype(BF16)
            kacc[h, span(t)] = dot(turned, q)
            vacc[h, span(t)] = dot(st[h, span(t)], g)
            if t > 0:
                chunk[1, h, t] = dot(qt[h, :, span(t)], g)
        return c

    lax.fori_loop(0, heads, backward_head, 0)
    for chunk_of, stop in enumerate(BACKWARD_STOPS):
        if stop >= heads:
            scan_middle(1, chunk_of, True)
    drain_out(0, False)
    drain_back(0, False)
    drain_out(1, True)
    remote(others, others, h_send, h_recv, "head", mine).wait_send()

    def last_head(h, c):
        cols = pl.ds(pl.multiple_of(h * D, D), D)
        after = incoming(1, h)
        for t in reversed(range(tiles)):
            late = after.astype(BF16)
            kg_ref[span(t), cols] = (kacc[h, span(t)] + dot_t(vb[h, span(t)], late)).astype(BF16)
            vg_ref[span(t), cols] = (vacc[h, span(t)] + dot(kb[h, span(t)], late)).astype(BF16)
            if t > 0:
                after = after + chunk[1, h, t]
        return c

    scan_end(1, 0, True)
    lax.fori_loop(0, group, last_head, 0, unroll=True)
    scan_end(1, 1, True)
    for i in range(group):
        h = group + i
        after = incoming(1, h)
        for t in reversed(range(tiles)):
            late_ref[i, t] = after.astype(BF16)
            if t > 0:
                after = after + chunk[1, h, t]
    drain_back(1, True)


def finish(
    group, tiles,
    qg_ref, kg_ref, vg_ref, kb, vb, kacc, vacc, late_ref,
    q_out, k_out, v_out,
    k_rest, v_rest, sems, rest_sems,
):
    done = pl.ds(0, group * D)
    copies = [
        pltpu.make_async_copy(qg_ref, q_out, sems.at[0]),
        pltpu.make_async_copy(kg_ref, k_out.at[:, done], sems.at[1]),
        pltpu.make_async_copy(vg_ref, v_out.at[:, done], sems.at[2]),
    ]
    for copy in copies:
        copy.start()
    for i in range(group):
        h = group + i
        for t in range(tiles):
            at = slice(t * TILE, (t + 1) * TILE)
            late = late_ref[i, t]
            k_rest[i, at] = (kacc[h, at] + dot_t(vb[h, at], late)).astype(BF16)
            v_rest[i, at] = (vacc[h, at] + dot(kb[h, at], late)).astype(BF16)
        cols = pl.ds(h * D, D)
        for which, (rest, out) in enumerate(((k_rest, k_out), (v_rest, v_out))):
            copy = pltpu.make_async_copy(rest.at[i], out.at[:, cols], rest_sems.at[which, i])
            copy.start()
            copies.append(copy)
    for copy in copies:
        copy.wait()


def shards(query, key_in, value, out_grad, gain):
    rows, width = query.shape
    heads = width // D
    tiles = rows // TILE
    blocks = lax.axis_size("seq")
    peers = lax.axis_size("head")
    part = D * heads // CHUNKS // blocks
    hbm = pl.BlockSpec(memory_space=pltpu.HBM)
    vmem = pl.BlockSpec(memory_space=pltpu.VMEM)
    dma = pltpu.SemaphoreType.DMA
    operands = [
        pltpu.with_memory_space_constraint(x, pltpu.HBM)
        for x in (query, key_in, value, out_grad, gain.reshape(heads, D))
    ]
    group = heads // CHUNKS
    held_shapes = [
        pltpu.VMEM((rows, width), BF16),
        pltpu.VMEM((rows, group * D), BF16),
        pltpu.VMEM((rows, group * D), BF16),
        pltpu.VMEM((heads, rows, D), BF16),
        pltpu.VMEM((heads, rows, D), BF16),
        pltpu.VMEM((heads, rows, D), F32),
        pltpu.VMEM((heads, rows, D), F32),
        pltpu.VMEM((group, tiles, D, D), BF16),
    ]
    held = pl.pallas_call(
        functools.partial(kernel, blocks, peers, rows, heads),
        out_shape=held_shapes,
        in_specs=[hbm] * 5,
        out_specs=[vmem] * len(held_shapes),
        scratch_shapes=[
            pltpu.VMEM((heads, D), F32),
            pltpu.VMEM((heads, rows, D), BF16),
            pltpu.VMEM((heads, rows, D), BF16),
            pltpu.VMEM((heads, rows, D), F32),
            pltpu.VMEM((heads, rows, D), BF16),
            pltpu.VMEM((heads, rows, TILE), BF16),
            pltpu.VMEM((heads, D, rows), BF16),
            pltpu.VMEM((2, heads, tiles, D, D), F32),
            pltpu.VMEM((2, CHUNKS, blocks, part, D), F32),
            pltpu.VMEM((2, CHUNKS, blocks, part, D), F32),
            pltpu.VMEM((2, CHUNKS, blocks, part, D), F32),
            pltpu.VMEM((2, CHUNKS, blocks, part, D), F32),
            pltpu.VMEM((heads, tiles, D, D), BF16),
            pltpu.VMEM((rows, D), F32),
            pltpu.VMEM((rows, D), F32),
            pltpu.VMEM((2 * STAT_ROWS, LANES), F32),
            pltpu.VMEM((peers, 2 * STAT_ROWS, LANES), F32),
            pltpu.VMEM((rows, LANES), F32),
            pltpu.VMEM((rows, LANES), F32),
            dma(()),
            dma((4, heads)),
            dma((2, CHUNKS)),
            dma((2, CHUNKS)),
            dma((2, CHUNKS)),
            dma((2, CHUNKS)),
            dma(()),
            dma(()),
        ],
        compiler_params=pltpu.CompilerParams(
            collective_id=0, has_side_effects=True, vmem_limit_bytes=40 * 1024 * 1024
        ),
    )(*operands)
    return pl.pallas_call(
        functools.partial(finish, group, tiles),
        out_shape=(jax.ShapeDtypeStruct((rows, width), BF16),) * 3,
        in_specs=[vmem] * len(held_shapes),
        out_specs=(hbm, hbm, hbm),
        scratch_shapes=[
            pltpu.VMEM((group, rows, D), BF16),
            pltpu.VMEM((group, rows, D), BF16),
            dma((3,)),
            dma((2, group)),
        ],
        compiler_params=pltpu.CompilerParams(vmem_limit_bytes=4 * 1024 * 1024),
    )(*held)


def solution(mesh):
    spec = P("seq", "head")
    return jax.shard_map(
        shards,
        mesh=mesh,
        in_specs=(spec, spec, spec, spec, P("head")),
        out_specs=(spec, spec, spec),
        check_vma=False,
    )
```

```python
import functools

import jax
import jax.numpy as jnp
from jax import lax
from jax.experimental import pallas as pl
from jax.experimental.pallas import tpu as pltpu
from jax.sharding import PartitionSpec as P

D = 128
TILE = 256
LANES = 128
EPS = 1e-06
SIDE = 4
CHUNKS = 2
STAT_ROWS = 8
FORWARD_STOPS = (4, 6)
BACKWARD_STOPS = (2, 4)
AWAY = (
    (2, 2), (2, 1), (1, 2), (2, 3), (3, 2), (1, 1), (3, 3), (1, 3),
    (3, 1), (2, 0), (0, 2), (0, 1), (1, 0), (0, 3), (3, 0),
)
MESH = pl.DeviceIdType.MESH
BF16 = jnp.bfloat16
F32 = jnp.float32


def dot(a, b):
    return jnp.dot(a, b, preferred_element_type=F32)


def dot_t(a, b):
    return lax.dot_general(a, b, (((1,), (1,)), ((), ())), preferred_element_type=F32)


def t_dot(a, b):
    return lax.dot_general(a, b, (((0,), (0,)), ((), ())), preferred_element_type=F32)


def thirds(x):
    high = x.astype(BF16)
    rest = x - high.astype(F32)
    middle = rest.astype(BF16)
    return high, middle, (rest - middle.astype(F32)).astype(BF16)


def remote(src, dst, send_sem, recv_sem, axis, peer):
    return pltpu.make_async_remote_copy(
        src_ref=src,
        dst_ref=dst,
        send_sem=send_sem,
        recv_sem=recv_sem,
        device_id={axis: peer},
        device_id_type=MESH,
    )


def kernel(
    blocks, peers, rows, heads,
    q_hbm, k_hbm, v_hbm, o_hbm, gain_hbm,
    qg_ref, kg_ref, vg_ref, kb, vb, kacc, vacc, late_ref,
    gain_ref, qb, ob, attn, gb, st, qt,
    local, arrived, prefix, entering, state, near, square, cross,
    stat, stats, inv_col, coef_col,
    gain_sem, in_sem, a_send, a_recv, b_send, b_recv, h_send, h_recv,
):
    me = lax.axis_index("seq")
    mine = lax.axis_index("head")
    tiles = rows // TILE
    group = heads // CHUNKS
    per_head = blocks // group
    part = D // per_head
    full = peers * heads * D
    row, col = me // SIDE, lax.rem(me, SIDE)

    def fetch(which, h):
        src = (q_hbm, k_hbm, v_hbm, o_hbm)[which]
        dst = (qb, kb, vb, ob)[which]
        return pltpu.make_async_copy(
            src.at[:, pl.ds(pl.multiple_of(h * D, D), D)], dst.at[h], in_sem.at[which, h]
        )

    def away(k):
        dx, dy = AWAY[k]
        return lax.rem(row + dx, SIDE) * SIDE + lax.rem(col + dy, SIDE)

    def start_kv(i, c):
        fetch(1, i).start()
        fetch(2, i).start()
        return c

    def start_q(i, c):
        fetch(0, i).start()
        return c

    def start_o(i, c):
        fetch(3, i).start()
        return c

    fetch_gain = pltpu.make_async_copy(gain_hbm, gain_ref, gain_sem)
    barrier = pltpu.get_barrier_semaphore()
    lax.fori_loop(0, group, start_kv, 0)
    for k in range(blocks - 1):
        pl.semaphore_signal(barrier, inc=1, device_id={"seq": away(k)}, device_id_type=MESH)
    lax.fori_loop(group, heads, start_kv, 0)
    for k in range(1, peers):
        pl.semaphore_signal(
            barrier, inc=1, device_id={"head": lax.rem(mine + k, peers)}, device_id_type=MESH
        )

    def slice_copy(scan, c, s):
        return remote(
            local.at[scan, c, s],
            arrived.at[scan, c, me],
            a_send.at[scan, c],
            a_recv.at[scan, c],
            "seq",
            s,
        )

    def send_slices(scan, c, last):
        @pl.when(me != last)
        def _():
            for k in range(blocks - 1):
                slice_copy(scan, c, away(k)).start()

        arrived[scan, c, me] = local[scan, c, me]

    def back_copy(scan, c, d):
        return remote(
            prefix.at[scan, c, d],
            entering.at[scan, c, me],
            b_send.at[scan, c],
            b_recv.at[scan, c],
            "seq",
            d,
        )

    def slices(ref, scan, c, count, send_sem, recv_sem):
        at = ref.at[scan, c, pl.ds(0, count)]
        return remote(at, at, send_sem.at[scan, c], recv_sem.at[scan, c], "seq", me)

    def scan_middle(scan, c, reverse):
        first = blocks - 1 if reverse else 0
        last = blocks - 1 - first
        for count, when in ((blocks - 2, me != last), (blocks - 1, me == last)):

            @pl.when(when)
            def _():
                slices(arrived, scan, c, count, a_send, a_recv).wait_recv()

        acc = None
        for i in range(blocks - 1):
            j = blocks - 1 - i if reverse else i
            acc = arrived[scan, c, j] if acc is None else acc + arrived[scan, c, j]
            prefix[scan, c, j - 1 if reverse else j + 1] = acc
        for k in range(blocks - 1):
            d = away(k)

            @pl.when(d != first)
            def _():
                back_copy(scan, c, d).start()

        @pl.when(me != first)
        def _():
            entering[scan, c, me] = prefix[scan, c, me]

        @pl.when(me == first)
        def _():
            entering[scan, c] = jnp.zeros((blocks, part, D), F32)

    def scan_end(scan, c, reverse):
        first = blocks - 1 if reverse else 0

        @pl.when(me != first)
        def _():
            slices(entering, scan, c, blocks - 1, b_send, b_recv).wait_recv()

    def drain_out(scan, reverse):
        last = 0 if reverse else blocks - 1
        for c in range(CHUNKS):

            @pl.when(me != last)
            def _():
                slices(local, scan, c, blocks - 1, a_send, a_recv).wait_send()

    def drain_back(scan, reverse):
        first = blocks - 1 if reverse else 0
        for c in range(CHUNKS):
            for count, when in ((blocks - 2, me != first), (blocks - 1, me == first)):

                @pl.when(when)
                def _():
                    slices(prefix, scan, c, count, b_send, b_recv).wait_send()

    def incoming(scan, h):
        c = h // group
        base = lax.rem(h, group) * per_head
        return entering[scan, c, pl.ds(base, per_head)].reshape(D, D)

    def keep_local(scan, h, total):
        c = h // group
        base = lax.rem(h, group) * per_head
        local[scan, c, pl.ds(base, per_head)] = total.reshape(per_head, part, D)

    def span(i):
        return slice(i * TILE, (i + 1) * TILE)

    pl.semaphore_wait(barrier, blocks - 1 + peers - 1)

    def kv_head(i, c):
        h = i
        fetch(1, h).wait()
        fetch(2, h).wait()
        keep_local(0, h, t_dot(kb[h], vb[h]))
        return c

    def kv_chunk(c, z):
        lax.fori_loop(c * group, (c + 1) * group, kv_head, 0, unroll=True)
        send_slices(0, c, blocks - 1)
        if c == 0:
            lax.fori_loop(0, heads, start_q, 0)
        return z

    for chunk_of in range(CHUNKS):
        kv_chunk(chunk_of, 0)
    lax.fori_loop(0, heads, start_o, 0)
    fetch_gain.start()

    at_or_below = lax.broadcasted_iota(jnp.int32, (TILE, TILE), 0) >= lax.broadcasted_iota(
        jnp.int32, (TILE, TILE), 1
    )
    at_or_above = lax.broadcasted_iota(jnp.int32, (TILE, TILE), 0) <= lax.broadcasted_iota(
        jnp.int32, (TILE, TILE), 1
    )

    def forward_head(h, c):
        for chunk_of, stop in enumerate(FORWARD_STOPS):

            @pl.when(h == stop)
            def _():
                scan_middle(0, chunk_of, False)

        fetch(0, h).wait()
        earlier = None
        for t in range(tiles):
            q, k, v = qb[h, span(t)], kb[h, span(t)], vb[h, span(t)]
            scores = jnp.where(at_or_below, dot_t(q, k), 0.0).astype(BF16)
            total = dot(scores, v)
            if t > 0:
                near[h, t - 1] = earlier.astype(BF16)
                total = total + dot(q, near[h, t - 1])
            attn[h, span(t)] = total
            st[h, span(t)] = jnp.where(at_or_above, dot_t(k, q), 0.0).astype(BF16)
            if t + 1 < tiles:
                own = t_dot(k, v)
                earlier = own if earlier is None else earlier + own
        qt[h] = qb[h].T
        return c

    lax.fori_loop(0, heads, forward_head, 0)
    for chunk_of, stop in enumerate(FORWARD_STOPS):
        if stop >= heads:
            scan_middle(0, chunk_of, False)

    fetch_gain.wait()
    square[...] = jnp.zeros_like(square)
    stat[...] = jnp.zeros_like(stat)
    cross[...] = jnp.zeros_like(cross)

    def attend_chunk(c):
        own = range(c * group, (c + 1) * group)
        for h in own:
            fetch(3, h).wait()
        scan_end(0, c, False)
        for h in own:
            state[h] = incoming(0, h).astype(BF16)
        for t in range(rows // LANES):
            at = slice(t * LANES, (t + 1) * LANES)
            squares, crosses = square[at], cross[at]
            for h in own:
                a = attn[h, at] + dot(qb[h, at], state[h])
                attn[h, at] = a
                squares = squares + a * a
                crosses = crosses + (gain_ref[h : h + 1, :] * ob[h, at].astype(F32)) * a
            if c + 1 < CHUNKS:
                square[at] = squares
                cross[at] = crosses
            else:
                stat[t : t + 1] = jnp.sum(squares.T, axis=0, keepdims=True)
                stat[STAT_ROWS + t : STAT_ROWS + t + 1] = jnp.sum(crosses.T, axis=0, keepdims=True)

    for chunk_of in range(CHUNKS):
        attend_chunk(chunk_of)
    def stat_copy(peer):
        return remote(stat, stats.at[mine], h_send, h_recv, "head", peer)

    for k in range(1, peers):
        stat_copy(lax.rem(mine + k, peers)).start()
    stats[mine] = stat[...]
    others = stats.at[pl.ds(0, peers - 1)]
    remote(others, others, h_send, h_recv, "head", mine).wait_recv()
    whole = stats[0]
    for p in range(1, peers):
        whole = whole + stats[p]
    inv = lax.rsqrt(whole[:STAT_ROWS] / full + EPS)
    coef = inv * inv * inv * (whole[STAT_ROWS:] / full)
    def grad_chunk(c):
        own = range(c * group, (c + 1) * group)
        for t in range(rows // LANES):
            at = slice(t * LANES, (t + 1) * LANES)
            if c == 0:
                scale = jnp.broadcast_to(inv[t : t + 1], (LANES, LANES)).T
                shift = jnp.broadcast_to(coef[t : t + 1], (LANES, LANES)).T
                inv_col[at] = scale
                coef_col[at] = shift
            else:
                scale, shift = inv_col[at], coef_col[at]
            for h in own:
                scaled = gain_ref[h : h + 1, :] * ob[h, at].astype(F32)
                gb[h, at] = (scale * scaled - attn[h, at] * shift).astype(BF16)
        for h in own:
            keep_local(1, h, dot(qt[h], gb[h]))
        send_slices(1, c, 0)

    for chunk_of in range(CHUNKS):
        grad_chunk(chunk_of)

    def backward_head(h, c):
        for chunk_of, stop in enumerate(BACKWARD_STOPS):

            @pl.when(h == stop)
            def _():
                scan_middle(1, chunk_of, True)

        cols = pl.ds(pl.multiple_of(h * D, D), D)
        later = None
        for t in reversed(range(tiles)):
            q, k, v, g = qb[h, span(t)], kb[h, span(t)], vb[h, span(t)], gb[h, span(t)]
            scores = jnp.where(at_or_below, dot_t(g, v), 0.0).astype(BF16)
            q_total = dot(scores, k) + dot_t(g, state[h])
            if t > 0:
                q_total = q_total + dot_t(g, near[h, t - 1])
            qg_ref[span(t), cols] = q_total.astype(BF16)
            turned = jnp.where(at_or_above, dot_t(v, g), 0.0).astype(BF16)
            k_total = dot(turned, q)
            v_total = dot(st[h, span(t)], g)
            if t + 1 < tiles:
                rounded = later.astype(BF16)
                k_total = k_total + dot_t(v, rounded)
                v_total = v_total + dot(k, rounded)
            kacc[h, span(t)] = k_total
            vacc[h, span(t)] = v_total
            if t > 0:
                own = dot(qt[h, :, span(t)], g)
                later = own if later is None else later + own
        return c

    lax.fori_loop(0, heads, backward_head, 0)
    for chunk_of, stop in enumerate(BACKWARD_STOPS):
        if stop >= heads:
            scan_middle(1, chunk_of, True)
    drain_out(0, False)
    drain_back(0, False)
    drain_out(1, True)
    remote(others, others, h_send, h_recv, "head", mine).wait_send()

    def last_head(h, c):
        cols = pl.ds(pl.multiple_of(h * D, D), D)
        late = incoming(1, h).astype(BF16)
        for t in range(tiles):
            kg_ref[span(t), cols] = (kacc[h, span(t)] + dot_t(vb[h, span(t)], late)).astype(BF16)
            vg_ref[span(t), cols] = (vacc[h, span(t)] + dot(kb[h, span(t)], late)).astype(BF16)
        return c

    scan_end(1, 0, True)
    lax.fori_loop(0, group, last_head, 0, unroll=True)
    scan_end(1, 1, True)
    for i in range(group):
        late_ref[i] = incoming(1, group + i).astype(BF16)
    drain_back(1, True)


def finish(
    group, tiles,
    qg_ref, kg_ref, vg_ref, kb, vb, kacc, vacc, late_ref,
    q_out, k_out, v_out,
    k_rest, v_rest, sems, rest_sems,
):
    done = pl.ds(0, group * D)
    copies = [
        pltpu.make_async_copy(qg_ref, q_out, sems.at[0]),
        pltpu.make_async_copy(kg_ref, k_out.at[:, done], sems.at[1]),
        pltpu.make_async_copy(vg_ref, v_out.at[:, done], sems.at[2]),
    ]
    for copy in copies:
        copy.start()
    for i in range(group):
        h = group + i
        late = late_ref[i]
        for t in range(tiles):
            at = slice(t * TILE, (t + 1) * TILE)
            k_rest[i, at] = (kacc[h, at] + dot_t(vb[h, at], late)).astype(BF16)
            v_rest[i, at] = (vacc[h, at] + dot(kb[h, at], late)).astype(BF16)
        cols = pl.ds(h * D, D)
        for which, (rest, out) in enumerate(((k_rest, k_out), (v_rest, v_out))):
            copy = pltpu.make_async_copy(rest.at[i], out.at[:, cols], rest_sems.at[which, i])
            copy.start()
            copies.append(copy)
    for copy in copies:
        copy.wait()


def shards(query, key_in, value, out_grad, gain):
    rows, width = query.shape
    heads = width // D
    tiles = rows // TILE
    blocks = lax.axis_size("seq")
    peers = lax.axis_size("head")
    part = D * heads // CHUNKS // blocks
    hbm = pl.BlockSpec(memory_space=pltpu.HBM)
    vmem = pl.BlockSpec(memory_space=pltpu.VMEM)
    dma = pltpu.SemaphoreType.DMA
    operands = [
        pltpu.with_memory_space_constraint(x, pltpu.HBM)
        for x in (query, key_in, value, out_grad, gain.reshape(heads, D))
    ]
    group = heads // CHUNKS
    held_shapes = [
        pltpu.VMEM((rows, width), BF16),
        pltpu.VMEM((rows, group * D), BF16),
        pltpu.VMEM((rows, group * D), BF16),
        pltpu.VMEM((heads, rows, D), BF16),
        pltpu.VMEM((heads, rows, D), BF16),
        pltpu.VMEM((heads, rows, D), F32),
        pltpu.VMEM((heads, rows, D), F32),
        pltpu.VMEM((group, D, D), BF16),
    ]
    held = pl.pallas_call(
        functools.partial(kernel, blocks, peers, rows, heads),
        out_shape=held_shapes,
        in_specs=[hbm] * 5,
        out_specs=[vmem] * len(held_shapes),
        scratch_shapes=[
            pltpu.VMEM((heads, D), F32),
            pltpu.VMEM((heads, rows, D), BF16),
            pltpu.VMEM((heads, rows, D), BF16),
            pltpu.VMEM((heads, rows, D), F32),
            pltpu.VMEM((heads, rows, D), BF16),
            pltpu.VMEM((heads, rows, TILE), BF16),
            pltpu.VMEM((heads, D, rows), BF16),
            pltpu.VMEM((2, CHUNKS, blocks, part, D), F32),
            pltpu.VMEM((2, CHUNKS, blocks, part, D), F32),
            pltpu.VMEM((2, CHUNKS, blocks, part, D), F32),
            pltpu.VMEM((2, CHUNKS, blocks, part, D), F32),
            pltpu.VMEM((heads, D, D), BF16),
            pltpu.VMEM((heads, tiles - 1, D, D), BF16),
            pltpu.VMEM((rows, D), F32),
            pltpu.VMEM((rows, D), F32),
            pltpu.VMEM((2 * STAT_ROWS, LANES), F32),
            pltpu.VMEM((peers, 2 * STAT_ROWS, LANES), F32),
            pltpu.VMEM((rows, LANES), F32),
            pltpu.VMEM((rows, LANES), F32),
            dma(()),
            dma((4, heads)),
            dma((2, CHUNKS)),
            dma((2, CHUNKS)),
            dma((2, CHUNKS)),
            dma((2, CHUNKS)),
            dma(()),
            dma(()),
        ],
        compiler_params=pltpu.CompilerParams(
            collective_id=0, has_side_effects=True, vmem_limit_bytes=40 * 1024 * 1024
        ),
    )(*operands)
    return pl.pallas_call(
        functools.partial(finish, group, tiles),
        out_shape=(jax.ShapeDtypeStruct((rows, width), BF16),) * 3,
        in_specs=[vmem] * len(held_shapes),
        out_specs=(hbm, hbm, hbm),
        scratch_shapes=[
            pltpu.VMEM((group, rows, D), BF16),
            pltpu.VMEM((group, rows, D), BF16),
            dma((3,)),
            dma((2, group)),
        ],
        compiler_params=pltpu.CompilerParams(vmem_limit_bytes=4 * 1024 * 1024),
    )(*held)


def solution(mesh):
    spec = P("seq", "head")
    return jax.shard_map(
        shards,
        mesh=mesh,
        in_specs=(spec, spec, spec, spec, P("head")),
        out_specs=(spec, spec, spec),
        check_vma=False,
    )
```
